32 devices in a mesh: seg: 4 (over z), slab: 8 (over y, x, core).
Axes of the slice: x: 2, y: 2, z: 4, core: 2. Of those that a mesh axis runs over, the one named last changes fastest.
Arguments:
- checkpoints: float32 [4, 32, 256, 512], P('seg', 'slab'), may hold values from 0 to 1
- control: float32 [4, 32, 256, 512], P('seg', 'slab'), may hold values from -4 to 4
- rate: float32 [32, 256, 512], P('slab'), may hold values from 0.25 to 2.5
- target: float32 [32, 256, 512], P('slab'), may hold values from 0 to 1
Outputs:
- new_checkpoints: float32 [4, 32, 256, 512], P('seg', 'slab')
- new_control: float32 [4, 32, 256, 512], P('seg', 'slab')
The draws below stay inside these ranges and needn't reach their ends.
All inputs are finite; a program needn't handle non-finite values.
Results may differ from the reference program's by a relative error of at most 0.00002.
Values sent between devices are 32-bit elements; how exact they have to be, the bound alone decides.
A program may use at most 128 MiB of HBM per device.

```python
import math
import jax
import jax.numpy as jnp

GX = 256
GY = 512
STEPS = 2
SEGS = 4
NZ = 32


def block_levels(stream_key, dims, split, low, largest):
    factor_of = 1.0
    for position, parts in split:
        steps = jax.random.uniform(jax.random.fold_in(jax.random.fold_in(stream_key, 6), position), (parts,), jnp.float32, low / len(split), largest / len(split))
        factor_of = factor_of * jnp.repeat(jnp.exp(steps), dims[position] // parts).reshape((-1,) + (1,) * (len(dims) - 1 - position))
    return factor_of


def normal_values(stream_key, dims, spread, bound, cuts=(), held_as=jnp.bfloat16):
    entries = spread * jax.random.normal(stream_key, dims, jnp.float32)
    if cuts:
        entries = entries * block_levels(stream_key, dims, cuts, -0.22, 0.18)
    return jnp.clip(entries, -bound, bound).astype(held_as)


def setup_inputs(seed: int = 0) -> dict:
    key_of = jax.random.split(jax.random.key(seed), 5)
    return {
        "checkpoints": jnp.clip(1.0 * jax.random.uniform(key_of[0], (SEGS, NZ, GX, GY), jnp.float32) ** block_levels(key_of[0], (SEGS, NZ, GX, GY), ((0, 4), (1, 8)), -0.2, 0.2), 0.0, 1.0),
        "control": normal_values(key_of[1], (SEGS, NZ, GX, GY), 0.5, 4.0, ((0, 4), (1, 8)), jnp.float32),
        "rate": jnp.clip(jnp.exp(math.log(2.5) - 2.3025851 * jax.random.uniform(key_of[2], (NZ, GX, GY), jnp.float32) ** block_levels(key_of[2], (NZ, GX, GY), ((0, 8),), -0.2, 0.2)), 0.25, 2.5),
        "target": jnp.clip(1.0 * jax.random.uniform(key_of[3], (NZ, GX, GY), jnp.float32) ** block_levels(key_of[3], (NZ, GX, GY), ((0, 8),), -0.2, 0.2), 0.0, 1.0),
    }


def laplace(field):
    padded = jnp.pad(field, 1)
    beside = padded[2:, 1:-1, 1:-1] + padded[:-2, 1:-1, 1:-1]
    beside = beside + padded[1:-1, 2:, 1:-1] + padded[1:-1, :-2, 1:-1]
    beside = beside + padded[1:-1, 1:-1, 2:] + padded[1:-1, 1:-1, :-2]
    return beside - 6.0 * field

def reference(checkpoints, control, rate, target):
    ends = []
    states = []
    for k in range(SEGS):
        state = checkpoints[k]
        path = [state]
        for t in range(STEPS):
            state = state + 0.1 * (laplace(state) + rate * state * (1.0 - state) + control[k])
            path.append(state)
        ends.append(state)
        states.append(path)
    grad_control = []
    grad_start = []
    prior = jnp.zeros_like(target)
    for k in range(SEGS):
        following = target if k == SEGS - 1 else checkpoints[k + 1]
        defect = ends[k] - following
        costate = defect
        total = jnp.zeros_like(target)
        for t in range(STEPS - 1, -1, -1):
            total = total + costate
            costate = costate + 0.1 * (laplace(costate) + rate * (1.0 - 2.0 * states[k][t]) * costate)
        grad_control.append(0.1 * total)
        grad_start.append(costate - prior)
        prior = defect
    grad_control = jnp.stack(grad_control)
    grad_start = jnp.stack(grad_start)
    squared = jnp.sum(grad_control * grad_control) + jnp.sum(grad_start * grad_start)
    count = 2.0 * SEGS * NZ * GX * GY
    scale = 0.5 / jnp.sqrt(squared / count + 1e-06)
    return (checkpoints - scale * grad_start, control - scale * grad_control)
```

```python
import functools

import jax
import jax.numpy as jnp
from jax import lax
from jax.experimental import pallas as pl
from jax.experimental.pallas import tpu as pltpu
from jax.sharding import PartitionSpec as P

CHUNKS = 8
PARTS = 8
TILE = 16
PAD = 8
LAG_B = 2
LAG_U = 6
HALVES = 2
QUARTERS = 4
LAG_0 = 2
MESH = pl.DeviceIdType.MESH


def kernel(
    n_seg, n_slab,
    cp, ctl_in, rate_in, target,
    u0, ctl, gs, gc, tot_out,
    u1, l2, l1, rat, end, cpn, prior, acc, slot_a, slot_b,
    sem_u0, sem_ctl, sem_rat, sem_alt_c, sem_alt_p,
    hs, hr, zs, zr, as_, ar, bs, br,
    passing, pr, ready,
):
    me_seg = lax.axis_index("seg")
    me_slab = lax.axis_index("slab")
    layers, rows, cols = cp.shape[1:]
    size = rows // CHUNKS
    tiles = size // TILE
    top = layers + 1
    has_low = me_slab > 0
    has_high = me_slab < n_slab - 1
    first = me_seg == 0
    last = me_seg == n_seg - 1

    def span(c):
        return pl.ds(pl.multiple_of(c * size, size), size)

    def padded(c):
        return pl.ds(pl.multiple_of(c * size + PAD, 8), size)

    odd = lax.rem(me_slab, 2)
    even = odd == 0
    is_odd = odd == 1

    def layer(j):
        return (1 - odd) * (layers - 1 - j) + odd * j

    close = layer(0)
    mids = [layer(j) for j in range(1, layers - 2)]
    next_far = layer(layers - 2)
    far = layer(layers - 1)
    mid_at = pl.ds(2 - odd, layers - 3)
    next_at = pl.ds(next_far, 1)
    close_at = pl.ds(close, 1)
    far_at = pl.ds(odd * (layers - 2), 2)

    begin = 2 * size + PAD
    pieces = ((0, begin), (begin, rows - begin))

    def loads(j):
        at, count = pieces[j]
        here = pl.ds(at, count)
        return (
            pltpu.make_async_copy(
                cp.at[0, :, here], u0.at[pl.ds(1, layers), pl.ds(at + PAD, count)], sem_u0.at[j]),
            pltpu.make_async_copy(ctl_in.at[0, :, here], ctl.at[:, here], sem_ctl.at[j]),
            pltpu.make_async_copy(rate_in.at[:, here], rat.at[:, here], sem_rat.at[j]),
        )

    def first_halo(j, up):
        at, count = pieces[j]
        return pltpu.make_async_remote_copy(
            cp.at[0, layers - 1 if up else 0, pl.ds(at, count)],
            u0.at[0 if up else top, pl.ds(at + PAD, count)],
            hs.at[0, int(up), j], hr.at[0, int(up), j],
            device_id={"slab": me_slab + (1 if up else -1)}, device_id_type=MESH)

    def send_first(j):
        @pl.when(even)
        def _():
            first_halo(j, True).start()

        @pl.when(is_odd)
        def _():
            first_halo(j, False).start()

    def wait_first(j):
        @pl.when(even)
        def _():
            first_halo(j, False).wait_recv()

        @pl.when(is_odd)
        def _():
            first_halo(j, True).wait_recv()

    def sent_first(j):
        @pl.when(even)
        def _():
            first_halo(j, True).wait_send()

        @pl.when(is_odd)
        def _():
            first_halo(j, False).wait_send()

    def alt_c():
        return pltpu.make_async_copy(target, cpn, sem_alt_c)

    def alt_p():
        return pltpu.make_async_copy(cp.at[0], prior, sem_alt_p)

    def halo_down(k, buf, c):
        src = cp.at[0, 0, span(c)] if buf is u0 else buf.at[1, padded(c)]
        return pltpu.make_async_remote_copy(
            src, buf.at[top, padded(c)], hs.at[k, 0, c], hr.at[k, 0, c],
            device_id={"slab": me_slab - 1}, device_id_type=MESH)

    def halo_up(k, buf, c):
        src = cp.at[0, layers - 1, span(c)] if buf is u0 else buf.at[layers, padded(c)]
        return pltpu.make_async_remote_copy(
            src, buf.at[0, padded(c)], hs.at[k, 1, c], hr.at[k, 1, c],
            device_id={"slab": me_slab + 1}, device_id_type=MESH)

    detour = n_slab == 8
    mid = n_slab // 2
    low_mid = me_slab == mid - 1
    high_mid = me_slab == mid

    def goes_round(c):
        return jnp.logical_and(lax.rem(c, 2) == 1, c < CHUNKS - 1)

    def to_relay(k, buf, c, up):
        z = layers if up else 1
        src = cp.at[0, z - 1, span(c)] if buf is u0 else buf.at[z, padded(c)]
        return pltpu.make_async_remote_copy(
            src, passing.at[k, span(c)], hs.at[k, int(up), c], pr.at[k, c],
            device_id={"slab": n_slab - 1 if up else 0}, device_id_type=MESH)

    def from_relay(k, buf, c, up):
        return pltpu.make_async_remote_copy(
            passing.at[k, span(c)], buf.at[0 if up else top, padded(c)],
            hs.at[k, int(up), c], hr.at[k, int(up), c],
            device_id={"slab": mid if up else mid - 1}, device_id_type=MESH)

    def relay(k, buf, c):
        if not detour:
            return

        @pl.when(jnp.logical_and(goes_round(c), jnp.logical_not(has_low)))
        def _():
            to_relay(k, buf, c, False).wait_recv()
            from_relay(k, buf, c, False).start()

        @pl.when(jnp.logical_and(goes_round(c), jnp.logical_not(has_high)))
        def _():
            to_relay(k, buf, c, True).wait_recv()
            from_relay(k, buf, c, True).start()

    far_low = jnp.logical_and(has_low, even)
    far_high = jnp.logical_and(has_high, is_odd)

    def send_close(k, buf, c):
        @pl.when(even)
        def _():
            halo_up(k, buf, c).start()

        @pl.when(is_odd)
        def _():
            halo_down(k, buf, c).start()

    def wait_close(k, buf, c):
        @pl.when(even)
        def _():
            halo_down(k, buf, c).wait_recv()

        @pl.when(is_odd)
        def _():
            halo_up(k, buf, c).wait_recv()

    def send_far(k, buf, c):
        low, high = far_low, far_high
        if detour:
            around = goes_round(c)
            low_round = jnp.logical_and(around, high_mid)
            high_round = jnp.logical_and(around, low_mid)

            @pl.when(low_round)
            def _():
                to_relay(k, buf, c, False).start()

            @pl.when(high_round)
            def _():
                to_relay(k, buf, c, True).start()

            low = jnp.logical_and(low, jnp.logical_not(low_round))
            high = jnp.logical_and(high, jnp.logical_not(high_round))

        @pl.when(low)
        def _():
            halo_down(k, buf, c).start()

        @pl.when(high)
        def _():
            halo_up(k, buf, c).start()

    def wait_far(k, buf, c):
        @pl.when(far_low)
        def _():
            halo_up(k, buf, c).wait_recv()

        @pl.when(far_high)
        def _():
            halo_down(k, buf, c).wait_recv()

    def sent_close(k, buf, c):
        @pl.when(even)
        def _():
            halo_up(k, buf, c).wait_send()

        @pl.when(is_odd)
        def _():
            halo_down(k, buf, c).wait_send()

    def sent_far(k, buf, c):
        @pl.when(far_low)
        def _():
            halo_down(k, buf, c).wait_send()

        @pl.when(far_high)
        def _():
            halo_up(k, buf, c).wait_send()

        if detour:
            @pl.when(jnp.logical_and(goes_round(c), jnp.logical_not(has_low)))
            def _():
                from_relay(k, buf, c, False).wait_send()

            @pl.when(jnp.logical_and(goes_round(c), jnp.logical_not(has_high)))
            def _():
                from_relay(k, buf, c, True).wait_send()

    rims = (0, layers - 1)
    ends = (mid_at, close_at, far_at)

    def send_mid(c):
        return pltpu.make_async_remote_copy(
            cp.at[0, mid_at, span(c)], cpn.at[mid_at, span(c)], zs.at[3, c], zr.at[3, c],
            device_id={"seg": me_seg - 1}, device_id_type=MESH)

    def send_rim(h, j):
        here = pl.ds(pl.multiple_of(h * (rows // HALVES), 8), rows // HALVES)
        return pltpu.make_async_remote_copy(
            cp.at[0, rims[j], here], cpn.at[rims[j], here],
            zs.at[4, 2 * h + j], zr.at[4, 2 * h + j],
            device_id={"seg": me_seg - 1}, device_id_type=MESH)

    def send_next(q):
        here = pl.ds(pl.multiple_of(q * (rows // QUARTERS), 8), rows // QUARTERS)
        return pltpu.make_async_remote_copy(
            cp.at[0, next_at, here], cpn.at[next_at, here], zs.at[5, q], zr.at[5, q],
            device_id={"seg": me_seg - 1}, device_id_type=MESH)

    def send_end(c, part):
        at = ends[part]
        return pltpu.make_async_remote_copy(
            end.at[at, span(c)], prior.at[at, span(c)], zs.at[part, c], zr.at[part, c],
            device_id={"seg": me_seg + 1}, device_id_type=MESH)

    barrier = pltpu.get_barrier_semaphore()
    slab_peers = [{"slab": lax.rem(me_slab + d, n_slab)} for d in range(1, n_slab)]
    seg_peers = [{"seg": lax.rem(me_seg + d, n_seg)} for d in range(1, n_seg)]
    both = [
        {"seg": lax.rem(me_seg + e, n_seg), "slab": lax.rem(me_slab + d, n_slab)}
        for e in range(1, n_seg) for d in range(1, n_slab)
    ]
    direct = n_seg * n_slab <= 32
    near = slab_peers + seg_peers
    peers = near + both
    for peer in near:
        pl.semaphore_signal(barrier, inc=1, device_id=peer, device_id_type=MESH)

    for copy in loads(0):
        copy.start()

    pl.semaphore_wait(barrier, len(near))

    send_first(0)
    for c in range(2):
        send_far(0, u0, c)

    @pl.when(jnp.logical_not(first))
    def _():
        for j in range(2):
            send_rim(0, j).start()

    for copy in loads(1):
        copy.start()
    send_first(1)

    @pl.loop(2, CHUNKS)
    def _(c):
        send_far(0, u0, c)

    edge = jnp.zeros((PAD, cols), jnp.float32)
    for buf in (u0, u1, l2, l1):
        for z in range(1, top):
            buf[z, pl.ds(0, PAD), :] = edge
            buf[z, pl.ds(rows + PAD, PAD), :] = edge

    def clear(z):
        @pl.loop(0, rows // PAD)
        def _(i):
            for buf in (u0, u1, l2, l1):
                buf[z, pl.ds(pl.multiple_of(i * PAD + PAD, 8), PAD), :] = edge

    @pl.when(jnp.logical_not(has_low))
    def _():
        clear(0)

    @pl.when(jnp.logical_not(has_high))
    def _():
        clear(top)

    acc[...] = jnp.zeros_like(acc)

    @pl.when(last)
    def _():
        alt_c().start()

    @pl.when(first)
    def _():
        alt_p().start()

    if direct:
        for peer in slab_peers:
            pl.semaphore_signal(ready, inc=1, device_id=peer, device_id_type=MESH)

    lane = lax.broadcasted_iota(jnp.int32, (TILE, cols), 1)
    at_left = lane == 0
    at_right = lane == cols - 1

    def laplace(buf, z, r):
        tall = buf[z, pl.ds(pl.multiple_of(r - PAD, 8), TILE + 2 * PAD), :]
        mid = tall[PAD:PAD + TILE]
        beside = buf[z + 1, pl.ds(r, TILE), :] + buf[z - 1, pl.ds(r, TILE), :]
        beside = beside + (tall[PAD + 1:PAD + 1 + TILE] + tall[PAD - 1:PAD - 1 + TILE])
        right = jnp.where(at_right, 0.0, pltpu.roll(mid, cols - 1, 1))
        left = jnp.where(at_left, 0.0, pltpu.roll(mid, 1, 1))
        return mid, beside + (right + left) - 6.0 * mid

    def each_tile(c, body, zs):
        def at_tile(i):
            r = pl.multiple_of(c * size + i * TILE, 8)
            for z in zs:
                body(z, r, pl.ds(r, TILE), pl.multiple_of(r + PAD, 8))

        if len(zs) > 2:
            pl.loop(0, tiles)(at_tile)
        else:
            for i in range(tiles):
                at_tile(i)

    def add_square(v):
        sq = v * v
        part = sq[:PAD]
        for i in range(1, TILE // PAD):
            part = part + sq[i * PAD:(i + 1) * PAD]
        acc[...] = acc[...] + part

    def forward(src, c, dst, zs):
        def body(z, r, at, p):
            u, lap = laplace(src, z + 1, p)
            new = u + 0.1 * (lap + rat[z, at, :] * u * (1.0 - u) + ctl[z, at, :])
            if dst is u1:
                u1[z + 1, pl.ds(p, TILE), :] = new
            else:
                end[z, at, :] = new
        each_tile(c, body, zs)

    def between(i, low, high):
        return pl.when(jnp.logical_and(i >= low, i < high))

    @pl.loop(0, CHUNKS + LAG_U)
    def _(i):
        for j in range(2):
            @pl.when(i == 2 * j)
            def _():
                for copy in loads(j):
                    copy.wait()
                wait_first(j)

        @pl.when(i < CHUNKS)
        def _():
            forward(u0, i, u1, [close, *mids, next_far])
            send_close(1, u1, i)

        @between(i, 1, CHUNKS + 1)
        def _():
            c = i - 1
            forward(u1, c, end, mids)

            @pl.when(jnp.logical_not(last))
            def _():
                send_end(c, 0).start()

        @between(i, 2, CHUNKS + 2)
        def _():
            c = i - 2
            wait_close(1, u1, c)
            forward(u1, c, end, [close])

            @pl.when(jnp.logical_not(last))
            def _():
                send_end(c, 1).start()

        @pl.when(jnp.logical_not(first))
        def _():
            for h in range(1, HALVES):
                @pl.when(i == h)
                def _():
                    for j in range(2):
                        send_rim(h, j).start()

            @between(i, HALVES, HALVES + QUARTERS)
            def _():
                send_next(i - HALVES).start()

            @pl.when(i >= LAG_U)
            def _():
                send_mid(i - LAG_U).start()

        @between(i, LAG_B - 1, CHUNKS + LAG_B - 1)
        def _():
            relay(0, u0, i - LAG_B + 1)

        @between(i, LAG_B, CHUNKS + LAG_B)
        def _():
            c = i - LAG_B
            wait_far(0, u0, c)
            forward(u0, c, u1, [far])
            send_far(1, u1, c)

        @between(i, LAG_B + 2, CHUNKS + LAG_B + 2)
        def _():
            relay(1, u1, i - LAG_B - 2)

        @pl.when(i >= LAG_U)
        def _():
            c = i - LAG_U
            wait_far(1, u1, c)
            forward(u1, c, end, [next_far, far])

            @pl.when(jnp.logical_not(last))
            def _():
                send_end(c, 2).start()

    def defect(c, zs):
        def body(z, r, at, p):
            l2[z + 1, pl.ds(p, TILE), :] = end[z, at, :] - cpn[z, at, :]
        each_tile(c, body, zs)

    @pl.when(last)
    def _():
        alt_c().wait()

    @pl.when(first)
    def _():
        alt_p().wait()

    @pl.loop(0, CHUNKS)
    def _(c):
        @pl.when(jnp.logical_and(jnp.logical_not(last), lax.rem(c, CHUNKS // HALVES) == 0))
        def _():
            for j in range(2):
                send_rim(c // (CHUNKS // HALVES), j).wait_recv()
        defect(c, rims)
        send_far(2, l2, c)
        send_close(2, l2, c)

    def do_l1(c, zs):
        def body(z, r, at, p):
            lam, lap = laplace(l2, z + 1, p)
            new = lam + 0.1 * (lap + rat[z, at, :] * (1.0 - 2.0 * u1[z + 1, pl.ds(p, TILE), :]) * lam)
            l1[z + 1, pl.ds(p, TILE), :] = new
            g = 0.1 * (lam + new)
            gc[z, at, :] = g
            add_square(g)
        each_tile(c, body, zs)

    def do_l0(c, zs):
        def body(z, r, at, p):
            lam, lap = laplace(l1, z + 1, p)
            start = u0[z + 1, pl.ds(p, TILE), :]
            gs[z, at, :] = lam + 0.1 * (lap + rat[z, at, :] * (1.0 - 2.0 * start) * lam)
        each_tile(c, body, zs)

    def do_start(c):
        @pl.when(jnp.logical_not(first))
        def _():
            for part in range(3):
                send_end(c, part).wait_recv()

        def body(z, r, at, p):
            g = gs[z, at, :] - (prior[z, at, :] - u0[z + 1, pl.ds(p, TILE), :])
            gs[z, at, :] = g
            add_square(g)
        each_tile(c, body, range(layers))

    relay(2, l2, 1)
    for j in range(2):
        sent_first(j)

    @pl.loop(0, CHUNKS)
    def _(c):
        @pl.when(jnp.logical_and(jnp.logical_not(last), lax.rem(c, CHUNKS // QUARTERS) == 0))
        def _():
            send_next(c // (CHUNKS // QUARTERS)).wait_recv()
        defect(c, [next_far])

        @pl.when(c < CHUNKS - 2)
        def _():
            relay(2, l2, c + 2)
        wait_far(2, l2, c)
        do_l1(c, [far])
        send_far(3, l1, c)

        @pl.when(c >= 1)
        def _():
            relay(3, l1, c - 1)
        sent_far(0, u0, c)
        sent_close(1, u1, c)
        sent_far(1, u1, c)

        @pl.when(jnp.logical_not(last))
        def _():
            for part in range(2):
                send_end(c, part).wait_send()

    @pl.loop(0, CHUNKS + LAG_0)
    def _(i):
        @pl.when(i < CHUNKS)
        def _():
            @pl.when(jnp.logical_not(last))
            def _():
                send_mid(i).wait_recv()
            defect(i, mids)
            wait_close(2, l2, i)
            do_l1(i, [close, next_far])
            send_close(3, l1, i)

        @between(i, 1, CHUNKS + 1)
        def _():
            do_l1(i - 1, mids)

        @pl.when(i < CHUNKS)
        def _():
            wait_far(3, l1, i)
            do_l0(i, [far])

        @between(i, 1, CHUNKS + 1)
        def _():
            do_l0(i - 1, [next_far])

        @pl.when(i >= LAG_0)
        def _():
            c = i - LAG_0
            wait_close(3, l1, c)
            do_l0(c, [close, *mids])
            do_start(c)

    def sent_rest():
        @pl.loop(0, CHUNKS)
        def _(c):
            for k, buf in ((2, l2), (3, l1)):
                sent_close(k, buf, c)
                sent_far(k, buf, c)

            @pl.when(jnp.logical_not(first))
            def _():
                send_mid(c).wait_send()

            @pl.when(jnp.logical_not(last))
            def _():
                send_end(c, 2).wait_send()

        @pl.when(jnp.logical_not(first))
        def _():
            for h in range(HALVES):
                for j in range(2):
                    send_rim(h, j).wait_send()
            for q in range(QUARTERS):
                send_next(q).wait_send()

    tile = acc[:, :128]
    for j in range(1, cols // 128):
        tile = tile + acc[:, j * 128:(j + 1) * 128]
    tile = jnp.sum(tile, axis=0, keepdims=True)

    def total(value, slots, owner, peers, ss, sr):
        count = len(peers)

        def copy(at, peer):
            return pltpu.make_async_remote_copy(
                slots.at[at], slots.at[at], ss, sr, device_id=peer, device_id_type=MESH)

        slots[owner] = value
        for peer in peers:
            copy(owner, peer).start()
        if slots is slot_a:
            sent_rest()
        everything = copy(pl.ds(0, count), peers[0])
        everything.wait_recv()
        result = slots[0]
        for j in range(1, count + 1):
            result = result + slots[j]
        return result, everything

    if direct:
        pl.semaphore_wait(ready, len(slab_peers))
        tile, sent_a = total(tile, slot_a, me_seg * n_slab + me_slab, peers, as_, ar)
        sent = [sent_a]
    else:
        tile, sent_a = total(tile, slot_a, me_slab, slab_peers, as_, ar)
        tile, sent_b = total(tile, slot_b, me_seg, seg_peers, bs, br)
        sent = [sent_a, sent_b]
    tot_out[...] = tile
    for copies in sent:
        copies.wait_send()


def update_kernel(
    count, u0, ctl, gs, gc, tot, new_cp, new_ctl, out_a, out_b, sem_a, sem_b
):
    layers, rows, cols = ctl.shape
    size = rows // PARTS
    sum_of = jnp.sum(tot[...], axis=1, keepdims=True)
    scale = jnp.broadcast_to(0.5 / jnp.sqrt(sum_of / count + 1e-06), (PAD, cols))

    def save(c):
        at = pl.ds(pl.multiple_of(c * size, size), size)
        return (
            pltpu.make_async_copy(out_a.at[:, at], new_cp.at[0, :, at], sem_a.at[c]),
            pltpu.make_async_copy(out_b.at[:, at], new_ctl.at[0, :, at], sem_b.at[c]),
        )

    @pl.loop(0, PARTS)
    def _(c):
        @pl.loop(0, size // PAD)
        def _(i):
            r = pl.multiple_of(c * size + i * PAD, 8)
            at = pl.ds(r, PAD)
            for z in range(layers):
                start = u0[z + 1, pl.ds(pl.multiple_of(r + PAD, 8), PAD), :]
                out_a[z, at, :] = start - scale * gs[z, at, :]
                out_b[z, at, :] = ctl[z, at, :] - scale * gc[z, at, :]
        for copy in save(c):
            copy.start()

    @pl.loop(0, PARTS)
    def _(c):
        for copy in save(c):
            copy.wait()


def per_device(checkpoints, control, rate, target):
    n_seg = lax.axis_size("seg")
    n_slab = lax.axis_size("slab")
    layers, rows, cols = rate.shape
    f32 = jnp.float32
    block = pltpu.VMEM((layers, rows, cols), f32)
    wide = pltpu.VMEM((layers + 2, rows + 2 * PAD, cols), f32)
    dma = pltpu.SemaphoreType.DMA
    hbm = pl.BlockSpec(memory_space=pltpu.HBM)
    vmem = pl.BlockSpec(memory_space=pltpu.VMEM)
    kept = pl.pallas_call(
        functools.partial(kernel, n_seg, n_slab),
        out_shape=(wide, block, block, block, pltpu.VMEM((1, 128), f32)),
        in_specs=[hbm] * 4,
        out_specs=(vmem,) * 5,
        scratch_shapes=[
            wide, wide, wide,
            block, block, block, block,
            pltpu.VMEM((PAD, cols), f32),
            pltpu.VMEM((n_slab * n_seg, 1, 128), f32),
            pltpu.VMEM((n_seg, 1, 128), f32),
            dma((2,)), dma((2,)), dma((2,)),
            dma(()), dma(()),
            dma((4, 2, CHUNKS)), dma((4, 2, CHUNKS)),
            dma((6, CHUNKS)), dma((6, CHUNKS)),
            dma(()), dma(()), dma(()), dma(()),
            pltpu.VMEM((4, rows, cols), f32), dma((4, CHUNKS)),
            pltpu.SemaphoreType.REGULAR,
        ],
        compiler_params=pltpu.CompilerParams(
            collective_id=0, has_side_effects=True, vmem_limit_bytes=50 << 20
        ),
        name="shooting",
    )(checkpoints, control, rate, target)
    count = 2.0 * n_seg * n_slab * rate.size
    return pl.pallas_call(
        functools.partial(update_kernel, count),
        out_shape=(
            jax.ShapeDtypeStruct(checkpoints.shape, f32),
            jax.ShapeDtypeStruct(control.shape, f32),
        ),
        in_specs=[vmem] * 5,
        out_specs=(hbm, hbm),
        scratch_shapes=[block, block, dma((PARTS,)), dma((PARTS,))],
        compiler_params=pltpu.CompilerParams(vmem_limit_bytes=8 << 20),
        name="update",
    )(*kept)


def solution(mesh):
    return jax.shard_map(
        per_device,
        mesh=mesh,
        in_specs=(
            P("seg", "slab", None, None),
            P("seg", "slab", None, None),
            P("slab", None, None),
            P("slab", None, None),
        ),
        out_specs=(P("seg", "slab", None, None), P("seg", "slab", None, None)),
        check_vma=False,
    )
```

```python
import functools

import jax
import jax.numpy as jnp
from jax import lax
from jax.experimental import pallas as pl
from jax.experimental.pallas import tpu as pltpu
from jax.sharding import PartitionSpec as P

CHUNKS = 8
PARTS = 8
TILE = 16
PAD = 8
LAG_B = 2
LAG_U = 6
HALVES = 2
QUARTERS = 4
LAG_0 = 2
MESH = pl.DeviceIdType.MESH


def kernel(
    n_seg, n_slab,
    cp, ctl_in, rate_in, target,
    u0, ctl, gs, gc, tot_out,
    u1, l2, l1, rat, end, cpn, prior, acc, slot_a, slot_b,
    sem_u0, sem_ctl, sem_rat, sem_alt_c, sem_alt_p,
    hs, hr, zs, zr_end, zr_mid, zr_rim, zr_next, as_, ar, bs, br,
    passing, pr, ready,
):
    me_seg = lax.axis_index("seg")
    me_slab = lax.axis_index("slab")
    layers, rows, cols = cp.shape[1:]
    size = rows // CHUNKS
    tiles = size // TILE
    top = layers + 1
    has_low = me_slab > 0
    has_high = me_slab < n_slab - 1
    first = me_seg == 0
    last = me_seg == n_seg - 1

    def span(c):
        return pl.ds(pl.multiple_of(c * size, size), size)

    def padded(c):
        return pl.ds(pl.multiple_of(c * size + PAD, 8), size)

    odd = lax.rem(me_slab, 2)
    even = odd == 0
    is_odd = odd == 1

    def layer(j):
        return (1 - odd) * (layers - 1 - j) + odd * j

    close = layer(0)
    mids = [layer(j) for j in range(1, layers - 2)]
    next_far = layer(layers - 2)
    far = layer(layers - 1)
    mid_at = pl.ds(2 - odd, layers - 3)
    next_at = pl.ds(next_far, 1)
    close_at = pl.ds(close, 1)
    far_at = pl.ds(odd * (layers - 2), 2)

    begin = 2 * size + PAD
    pieces = ((0, begin), (begin, rows - begin))

    def loads(j):
        at, count = pieces[j]
        here = pl.ds(at, count)
        return (
            pltpu.make_async_copy(
                cp.at[0, :, here], u0.at[pl.ds(1, layers), pl.ds(at + PAD, count)], sem_u0.at[j]),
            pltpu.make_async_copy(ctl_in.at[0, :, here], ctl.at[:, here], sem_ctl.at[j]),
            pltpu.make_async_copy(rate_in.at[:, here], rat.at[:, here], sem_rat.at[j]),
        )

    def first_halo(j, up):
        at, count = pieces[j]
        return pltpu.make_async_remote_copy(
            cp.at[0, layers - 1 if up else 0, pl.ds(at, count)],
            u0.at[0 if up else top, pl.ds(at + PAD, count)],
            hs.at[0], hr.at[0, int(up), j],
            device_id={"slab": me_slab + (1 if up else -1)}, device_id_type=MESH)

    def send_first(j):
        @pl.when(even)
        def _():
            first_halo(j, True).start()

        @pl.when(is_odd)
        def _():
            first_halo(j, False).start()

    def wait_first(j):
        @pl.when(even)
        def _():
            first_halo(j, False).wait_recv()

        @pl.when(is_odd)
        def _():
            first_halo(j, True).wait_recv()

    def alt_c():
        return pltpu.make_async_copy(target, cpn, sem_alt_c)

    def alt_p():
        return pltpu.make_async_copy(cp.at[0], prior, sem_alt_p)

    def halo_down(k, buf, c):
        src = cp.at[0, 0, span(c)] if buf is u0 else buf.at[1, padded(c)]
        return pltpu.make_async_remote_copy(
            src, buf.at[top, padded(c)], hs.at[1 - odd], hr.at[k % 2, 0, c],
            device_id={"slab": me_slab - 1}, device_id_type=MESH)

    def halo_up(k, buf, c):
        src = cp.at[0, layers - 1, span(c)] if buf is u0 else buf.at[layers, padded(c)]
        return pltpu.make_async_remote_copy(
            src, buf.at[0, padded(c)], hs.at[odd], hr.at[k % 2, 1, c],
            device_id={"slab": me_slab + 1}, device_id_type=MESH)

    detour = n_slab == 8
    mid = n_slab // 2
    low_mid = me_slab == mid - 1
    high_mid = me_slab == mid

    def goes_round(c):
        return jnp.logical_and(lax.rem(c, 2) == 1, c < CHUNKS - 1)

    def to_relay(k, buf, c, up):
        z = layers if up else 1
        src = cp.at[0, z - 1, span(c)] if buf is u0 else buf.at[z, padded(c)]
        return pltpu.make_async_remote_copy(
            src, passing.at[k, span(c)], hs.at[1], pr.at[k % 2, c // 2],
            device_id={"slab": n_slab - 1 if up else 0}, device_id_type=MESH)

    def from_relay(k, buf, c, up):
        return pltpu.make_async_remote_copy(
            passing.at[k, span(c)], buf.at[0 if up else top, padded(c)],
            hs.at[2], hr.at[k % 2, int(up), c],
            device_id={"slab": mid if up else mid - 1}, device_id_type=MESH)

    def relay(k, buf, c):
        if not detour:
            return

        @pl.when(jnp.logical_and(goes_round(c), jnp.logical_not(has_low)))
        def _():
            to_relay(k, buf, c, False).wait_recv()
            from_relay(k, buf, c, False).start()

        @pl.when(jnp.logical_and(goes_round(c), jnp.logical_not(has_high)))
        def _():
            to_relay(k, buf, c, True).wait_recv()
            from_relay(k, buf, c, True).start()

    far_low = jnp.logical_and(has_low, even)
    far_high = jnp.logical_and(has_high, is_odd)

    def send_close(k, buf, c):
        @pl.when(even)
        def _():
            halo_up(k, buf, c).start()

        @pl.when(is_odd)
        def _():
            halo_down(k, buf, c).start()

    def wait_close(k, buf, c):
        @pl.when(even)
        def _():
            halo_down(k, buf, c).wait_recv()

        @pl.when(is_odd)
        def _():
            halo_up(k, buf, c).wait_recv()

    def send_far(k, buf, c):
        low, high = far_low, far_high
        if detour:
            around = goes_round(c)
            low_round = jnp.logical_and(around, high_mid)
            high_round = jnp.logical_and(around, low_mid)

            @pl.when(low_round)
            def _():
                to_relay(k, buf, c, False).start()

            @pl.when(high_round)
            def _():
                to_relay(k, buf, c, True).start()

            low = jnp.logical_and(low, jnp.logical_not(low_round))
            high = jnp.logical_and(high, jnp.logical_not(high_round))

        @pl.when(low)
        def _():
            halo_down(k, buf, c).start()

        @pl.when(high)
        def _():
            halo_up(k, buf, c).start()

    def wait_far(k, buf, c):
        @pl.when(far_low)
        def _():
            halo_up(k, buf, c).wait_recv()

        @pl.when(far_high)
        def _():
            halo_down(k, buf, c).wait_recv()

    def sent_halos():
        def taken(ref, sem):
            pltpu.make_async_remote_copy(
                ref, ref, sem, hr.at[0, 0, 0],
                device_id={"slab": lax.rem(me_slab + 1, n_slab)}, device_id_type=MESH).wait_send()

        taken(passing, hs.at[0])

        @pl.when(jnp.logical_or(far_low, far_high))
        def _():
            taken(passing, hs.at[1])

        if detour:
            @pl.when(jnp.logical_or(jnp.logical_not(has_low), jnp.logical_not(has_high)))
            def _():
                taken(passing.at[:, pl.ds(0, (CHUNKS - 1) // 2 * size)], hs.at[2])

    rims = (0, layers - 1)
    ends = (mid_at, close_at, far_at)

    def back(src, dst, sem):
        return pltpu.make_async_remote_copy(
            src, dst, zs.at[0], sem, device_id={"seg": me_seg - 1}, device_id_type=MESH)

    def onward(at, here, sem):
        return pltpu.make_async_remote_copy(
            end.at[at, here], prior.at[at, here], zs.at[1], sem,
            device_id={"seg": me_seg + 1}, device_id_type=MESH)

    def send_mid(c):
        return back(cp.at[0, mid_at, span(c)], cpn.at[mid_at, span(c)], zr_mid.at[c])

    def half(h):
        return pl.ds(pl.multiple_of(h * (rows // HALVES), 8), rows // HALVES)

    def send_rim(h, j):
        return back(cp.at[0, rims[j], half(h)], cpn.at[rims[j], half(h)], zr_rim.at[h])

    def both_rims(h):
        two = pl.ds(0, 2)
        return back(cp.at[0, two, half(h)], cpn.at[two, half(h)], zr_rim.at[h])

    def send_next(q):
        here = pl.ds(pl.multiple_of(q * (rows // QUARTERS), 8), rows // QUARTERS)
        return back(cp.at[0, next_at, here], cpn.at[next_at, here], zr_next.at[q])

    def send_end(c, part):
        return onward(ends[part], span(c), zr_end.at[c])

    def whole_end(c):
        return onward(pl.ds(0, layers), span(c), zr_end.at[c])

    barrier = pltpu.get_barrier_semaphore()
    slab_peers = [{"slab": lax.rem(me_slab + d, n_slab)} for d in range(1, n_slab)]
    seg_peers = [{"seg": lax.rem(me_seg + d, n_seg)} for d in range(1, n_seg)]
    both = [
        {"seg": lax.rem(me_seg + e, n_seg), "slab": lax.rem(me_slab + d, n_slab)}
        for e in range(1, n_seg) for d in range(1, n_slab)
    ]
    direct = n_seg * n_slab <= 32
    near = slab_peers + seg_peers
    peers = near + both
    for peer in near:
        pl.semaphore_signal(barrier, inc=1, device_id=peer, device_id_type=MESH)

    for copy in loads(0):
        copy.start()

    pl.semaphore_wait(barrier, len(near))

    send_first(0)
    for c in range(2):
        send_far(0, u0, c)

    @pl.when(jnp.logical_not(first))
    def _():
        for j in range(2):
            send_rim(0, j).start()

    for copy in loads(1):
        copy.start()
    send_first(1)

    @pl.loop(2, CHUNKS)
    def _(c):
        send_far(0, u0, c)

    edge = jnp.zeros((PAD, cols), jnp.float32)
    for buf in (u0, u1, l2, l1):
        for z in range(1, top):
            buf[z, pl.ds(0, PAD), :] = edge
            buf[z, pl.ds(rows + PAD, PAD), :] = edge

    def clear(z):
        @pl.loop(0, rows // PAD)
        def _(i):
            for buf in (u0, u1, l2, l1):
                buf[z, pl.ds(pl.multiple_of(i * PAD + PAD, 8), PAD), :] = edge

    @pl.when(jnp.logical_not(has_low))
    def _():
        clear(0)

    @pl.when(jnp.logical_not(has_high))
    def _():
        clear(top)

    acc[...] = jnp.zeros_like(acc)

    @pl.when(last)
    def _():
        alt_c().start()

    @pl.when(first)
    def _():
        alt_p().start()

    if direct:
        for peer in slab_peers:
            pl.semaphore_signal(ready, inc=1, device_id=peer, device_id_type=MESH)

    lane = lax.broadcasted_iota(jnp.int32, (TILE, cols), 1)
    at_left = lane == 0
    at_right = lane == cols - 1

    def laplace(buf, z, r):
        tall = buf[z, pl.ds(pl.multiple_of(r - PAD, 8), TILE + 2 * PAD), :]
        mid = tall[PAD:PAD + TILE]
        beside = buf[z + 1, pl.ds(r, TILE), :] + buf[z - 1, pl.ds(r, TILE), :]
        beside = beside + (tall[PAD + 1:PAD + 1 + TILE] + tall[PAD - 1:PAD - 1 + TILE])
        right = jnp.where(at_right, 0.0, pltpu.roll(mid, cols - 1, 1))
        left = jnp.where(at_left, 0.0, pltpu.roll(mid, 1, 1))
        return mid, beside + (right + left) - 6.0 * mid

    def each_tile(c, body, zs):
        def at_tile(i):
            r = pl.multiple_of(c * size + i * TILE, 8)
            for z in zs:
                body(z, r, pl.ds(r, TILE), pl.multiple_of(r + PAD, 8))

        if len(zs) > 2:
            pl.loop(0, tiles)(at_tile)
        else:
            for i in range(tiles):
                at_tile(i)

    def add_square(v):
        sq = v * v
        part = sq[:PAD]
        for i in range(1, TILE // PAD):
            part = part + sq[i * PAD:(i + 1) * PAD]
        acc[...] = acc[...] + part

    def forward(src, c, dst, zs):
        def body(z, r, at, p):
            u, lap = laplace(src, z + 1, p)
            new = u + 0.1 * (lap + rat[z, at, :] * u * (1.0 - u) + ctl[z, at, :])
            if dst is u1:
                u1[z + 1, pl.ds(p, TILE), :] = new
            else:
                end[z, at, :] = new
        each_tile(c, body, zs)

    def between(i, low, high):
        return pl.when(jnp.logical_and(i >= low, i < high))

    @pl.loop(0, CHUNKS + LAG_U)
    def _(i):
        for j in range(2):
            @pl.when(i == 2 * j)
            def _():
                for copy in loads(j):
                    copy.wait()
                wait_first(j)

        @pl.when(i < CHUNKS)
        def _():
            forward(u0, i, u1, [close, *mids, next_far])
            send_close(1, u1, i)

        @between(i, 1, CHUNKS + 1)
        def _():
            c = i - 1
            forward(u1, c, end, mids)

            @pl.when(jnp.logical_not(last))
            def _():
                send_end(c, 0).start()

        @between(i, 2, CHUNKS + 2)
        def _():
            c = i - 2
            wait_close(1, u1, c)
            forward(u1, c, end, [close])

            @pl.when(jnp.logical_not(last))
            def _():
                send_end(c, 1).start()

        @pl.when(jnp.logical_not(first))
        def _():
            for h in range(1, HALVES):
                @pl.when(i == h)
                def _():
                    for j in range(2):
                        send_rim(h, j).start()

            @between(i, HALVES, HALVES + QUARTERS)
            def _():
                send_next(i - HALVES).start()

            @pl.when(i >= LAG_U)
            def _():
                send_mid(i - LAG_U).start()

        @between(i, LAG_B - 1, CHUNKS + LAG_B - 1)
        def _():
            relay(0, u0, i - LAG_B + 1)

        @between(i, LAG_B, CHUNKS + LAG_B)
        def _():
            c = i - LAG_B
            wait_far(0, u0, c)
            forward(u0, c, u1, [far])
            send_far(1, u1, c)

        @between(i, LAG_B + 2, CHUNKS + LAG_B + 2)
        def _():
            relay(1, u1, i - LAG_B - 2)

        @pl.when(i >= LAG_U)
        def _():
            c = i - LAG_U
            wait_far(1, u1, c)
            forward(u1, c, end, [next_far, far])

            @pl.when(jnp.logical_not(last))
            def _():
                send_end(c, 2).start()

    def defect(c, zs):
        def body(z, r, at, p):
            l2[z + 1, pl.ds(p, TILE), :] = end[z, at, :] - cpn[z, at, :]
        each_tile(c, body, zs)

    @pl.when(last)
    def _():
        alt_c().wait()

    @pl.when(first)
    def _():
        alt_p().wait()

    @pl.loop(0, CHUNKS)
    def _(c):
        @pl.when(jnp.logical_and(jnp.logical_not(last), lax.rem(c, CHUNKS // HALVES) == 0))
        def _():
            both_rims(c // (CHUNKS // HALVES)).wait_recv()
        defect(c, rims)
        send_far(2, l2, c)
        send_close(2, l2, c)

    def do_l1(c, zs):
        def body(z, r, at, p):
            lam, lap = laplace(l2, z + 1, p)
            new = lam + 0.1 * (lap + rat[z, at, :] * (1.0 - 2.0 * u1[z + 1, pl.ds(p, TILE), :]) * lam)
            l1[z + 1, pl.ds(p, TILE), :] = new
            g = 0.1 * (lam + new)
            gc[z, at, :] = g
            add_square(g)
        each_tile(c, body, zs)

    def do_l0(c, zs):
        def body(z, r, at, p):
            lam, lap = laplace(l1, z + 1, p)
            start = u0[z + 1, pl.ds(p, TILE), :]
            gs[z, at, :] = lam + 0.1 * (lap + rat[z, at, :] * (1.0 - 2.0 * start) * lam)
        each_tile(c, body, zs)

    def do_start(c):
        @pl.when(jnp.logical_not(first))
        def _():
            whole_end(c).wait_recv()

        def body(z, r, at, p):
            g = gs[z, at, :] - (prior[z, at, :] - u0[z + 1, pl.ds(p, TILE), :])
            gs[z, at, :] = g
            add_square(g)
        each_tile(c, body, range(layers))

    relay(2, l2, 1)

    @pl.loop(0, CHUNKS)
    def _(c):
        @pl.when(jnp.logical_and(jnp.logical_not(last), lax.rem(c, CHUNKS // QUARTERS) == 0))
        def _():
            send_next(c // (CHUNKS // QUARTERS)).wait_recv()
        defect(c, [next_far])

        @pl.when(c < CHUNKS - 2)
        def _():
            relay(2, l2, c + 2)
        wait_far(2, l2, c)
        do_l1(c, [far])
        send_far(3, l1, c)

        @pl.when(c >= 1)
        def _():
            relay(3, l1, c - 1)

    @pl.loop(0, CHUNKS + LAG_0)
    def _(i):
        @pl.when(i < CHUNKS)
        def _():
            @pl.when(jnp.logical_not(last))
            def _():
                send_mid(i).wait_recv()
            defect(i, mids)
            wait_close(2, l2, i)
            do_l1(i, [close, next_far])
            send_close(3, l1, i)

        @between(i, 1, CHUNKS + 1)
        def _():
            do_l1(i - 1, mids)

        @pl.when(i < CHUNKS)
        def _():
            wait_far(3, l1, i)
            do_l0(i, [far])

        @between(i, 1, CHUNKS + 1)
        def _():
            do_l0(i - 1, [next_far])

        @pl.when(i >= LAG_0)
        def _():
            c = i - LAG_0
            wait_close(3, l1, c)
            do_l0(c, [close, *mids])
            do_start(c)

    def sent_all():
        sent_halos()

        @pl.when(jnp.logical_not(first))
        def _():
            back(cp.at[0], cpn, zr_mid.at[0]).wait_send()

        @pl.when(jnp.logical_not(last))
        def _():
            onward(pl.ds(0, layers), pl.ds(0, rows), zr_end.at[0]).wait_send()

    tile = acc[:, :128]
    for j in range(1, cols // 128):
        tile = tile + acc[:, j * 128:(j + 1) * 128]
    tile = jnp.sum(tile, axis=0, keepdims=True)

    def total(value, slots, owner, peers, ss, sr):
        count = len(peers)

        def copy(at, peer):
            return pltpu.make_async_remote_copy(
                slots.at[at], slots.at[at], ss, sr, device_id=peer, device_id_type=MESH)

        slots[owner] = value
        for peer in peers:
            copy(owner, peer).start()
        if slots is slot_a:
            sent_all()
        everything = copy(pl.ds(0, count), peers[0])
        everything.wait_recv()
        result = slots[0]
        for j in range(1, count + 1):
            result = result + slots[j]
        return result, everything

    if direct:
        pl.semaphore_wait(ready, len(slab_peers))
        tile, sent_a = total(tile, slot_a, me_seg * n_slab + me_slab, peers, as_, ar)
        sent = [sent_a]
    else:
        tile, sent_a = total(tile, slot_a, me_slab, slab_peers, as_, ar)
        tile, sent_b = total(tile, slot_b, me_seg, seg_peers, bs, br)
        sent = [sent_a, sent_b]
    tot_out[...] = tile
    for copies in sent:
        copies.wait_send()


def update_kernel(
    count, u0, ctl, gs, gc, tot, new_cp, new_ctl, out_a, out_b, sem_a, sem_b
):
    layers, rows, cols = ctl.shape
    size = rows // PARTS
    sum_of = jnp.sum(tot[...], axis=1, keepdims=True)
    scale = jnp.broadcast_to(0.5 / jnp.sqrt(sum_of / count + 1e-06), (PAD, cols))

    def save(c):
        at = pl.ds(pl.multiple_of(c * size, size), size)
        return (
            pltpu.make_async_copy(out_a.at[:, at], new_cp.at[0, :, at], sem_a),
            pltpu.make_async_copy(out_b.at[:, at], new_ctl.at[0, :, at], sem_b),
        )

    @pl.loop(0, PARTS)
    def _(c):
        @pl.loop(0, size // PAD)
        def _(i):
            r = pl.multiple_of(c * size + i * PAD, 8)
            at = pl.ds(r, PAD)
            for z in range(layers):
                start = u0[z + 1, pl.ds(pl.multiple_of(r + PAD, 8), PAD), :]
                out_a[z, at, :] = start - scale * gs[z, at, :]
                out_b[z, at, :] = ctl[z, at, :] - scale * gc[z, at, :]
        for copy in save(c):
            copy.start()

    pltpu.make_async_copy(out_a, new_cp.at[0], sem_a).wait()
    pltpu.make_async_copy(out_b, new_ctl.at[0], sem_b).wait()


def per_device(checkpoints, control, rate, target):
    n_seg = lax.axis_size("seg")
    n_slab = lax.axis_size("slab")
    layers, rows, cols = rate.shape
    f32 = jnp.float32
    block = pltpu.VMEM((layers, rows, cols), f32)
    wide = pltpu.VMEM((layers + 2, rows + 2 * PAD, cols), f32)
    dma = pltpu.SemaphoreType.DMA
    hbm = pl.BlockSpec(memory_space=pltpu.HBM)
    vmem = pl.BlockSpec(memory_space=pltpu.VMEM)
    kept = pl.pallas_call(
        functools.partial(kernel, n_seg, n_slab),
        out_shape=(wide, block, block, block, pltpu.VMEM((1, 128), f32)),
        in_specs=[hbm] * 4,
        out_specs=(vmem,) * 5,
        scratch_shapes=[
            wide, wide, wide,
            block, block, block, block,
            pltpu.VMEM((PAD, cols), f32),
            pltpu.VMEM((n_slab * n_seg, 1, 128), f32),
            pltpu.VMEM((n_seg, 1, 128), f32),
            dma((2,)), dma((2,)), dma((2,)),
            dma(()), dma(()),
            dma((3,)), dma((2, 2, CHUNKS)),
            dma((2,)), dma((CHUNKS,)), dma((CHUNKS,)), dma((HALVES,)), dma((QUARTERS,)),
            dma(()), dma(()), dma(()), dma(()),
            pltpu.VMEM((4, rows, cols), f32), dma((2, CHUNKS // 2)),
            pltpu.SemaphoreType.REGULAR,
        ],
        compiler_params=pltpu.CompilerParams(
            collective_id=0, has_side_effects=True, vmem_limit_bytes=50 << 20
        ),
        name="shooting",
    )(checkpoints, control, rate, target)
    count = 2.0 * n_seg * n_slab * rate.size
    return pl.pallas_call(
        functools.partial(update_kernel, count),
        out_shape=(
            jax.ShapeDtypeStruct(checkpoints.shape, f32),
            jax.ShapeDtypeStruct(control.shape, f32),
        ),
        in_specs=[vmem] * 5,
        out_specs=(hbm, hbm),
        scratch_shapes=[block, block, dma(()), dma(())],
        compiler_params=pltpu.CompilerParams(vmem_limit_bytes=8 << 20),
        name="update",
    )(*kept)


def solution(mesh):
    return jax.shard_map(
        per_device,
        mesh=mesh,
        in_specs=(
            P("seg", "slab", None, None),
            P("seg", "slab", None, None),
            P("slab", None, None),
            P("slab", None, None),
        ),
        out_specs=(P("seg", "slab", None, None), P("seg", "slab", None, None)),
        check_vma=False,
    )
```

```python
import functools

import jax
import jax.numpy as jnp
from jax import lax
from jax.experimental import pallas as pl
from jax.experimental.pallas import tpu as pltpu
from jax.sharding import PartitionSpec as P

CHUNKS = 8
PARTS = 8
TILE = 16
PAD = 8
LAG_B = 2
LAG_U = 6
HALVES = 2
QUARTERS = 4
LAG_0 = 2
MESH = pl.DeviceIdType.MESH


def kernel(
    n_seg, n_slab,
    cp, ctl_in, rate_in, target,
    u0, ctl, gs, gc, tot_out,
    u1, l2, l1, rat, end, cpn, prior, acc, slot_a, slot_b,
    sem_u0, sem_ctl, sem_rat, sem_alt_c, sem_alt_p,
    hs, hr, zs, zr_end, zr_near, zr_mid, zr_rim, zr_next, as_, ar, bs, br,
    passing, pr, ready,
):
    me_seg = lax.axis_index("seg")
    me_slab = lax.axis_index("slab")
    layers, rows, cols = cp.shape[1:]
    size = rows // CHUNKS
    tiles = size // TILE
    top = layers + 1
    has_low = me_slab > 0
    has_high = me_slab < n_slab - 1
    first = me_seg == 0
    last = me_seg == n_seg - 1

    def span(c):
        return pl.ds(pl.multiple_of(c * size, size), size)

    def padded(c):
        return pl.ds(pl.multiple_of(c * size + PAD, 8), size)

    odd = lax.rem(me_slab, 2)
    even = odd == 0
    is_odd = odd == 1

    def layer(j):
        return (1 - odd) * (layers - 1 - j) + odd * j

    close = layer(0)
    mids = [layer(j) for j in range(1, layers - 2)]
    next_far = layer(layers - 2)
    far = layer(layers - 1)
    mid_at = pl.ds(2 - odd, layers - 3)
    next_at = pl.ds(next_far, 1)
    close_at = pl.ds(close, 1)
    far_at = pl.ds(odd * (layers - 2), 2)

    near_at = pl.ds(2 * (1 - odd), layers - 2)

    begin = size + PAD
    later = min(begin + 2 * size, rows)
    pieces = ((0, begin), (begin, later - begin), (later, rows - later))

    def loads(j):
        at, count = pieces[j]
        here = pl.ds(at, count)
        return (
            pltpu.make_async_copy(
                cp.at[0, :, here], u0.at[pl.ds(1, layers), pl.ds(at + PAD, count)], sem_u0.at[j]),
            pltpu.make_async_copy(ctl_in.at[0, :, here], ctl.at[:, here], sem_ctl.at[j]),
            pltpu.make_async_copy(rate_in.at[:, here], rat.at[:, here], sem_rat.at[j]),
        )

    def first_halo(j, up):
        at, count = pieces[j]
        return pltpu.make_async_remote_copy(
            cp.at[0, layers - 1 if up else 0, pl.ds(at, count)],
            u0.at[0 if up else top, pl.ds(at + PAD, count)],
            hs.at[0], hr.at[0, int(up), j],
            device_id={"slab": me_slab + (1 if up else -1)}, device_id_type=MESH)

    def send_first(j):
        @pl.when(even)
        def _():
            first_halo(j, True).start()

        @pl.when(is_odd)
        def _():
            first_halo(j, False).start()

    def wait_first(j):
        @pl.when(even)
        def _():
            first_halo(j, False).wait_recv()

        @pl.when(is_odd)
        def _():
            first_halo(j, True).wait_recv()

    def alt_c():
        return pltpu.make_async_copy(target, cpn, sem_alt_c)

    def alt_p():
        return pltpu.make_async_copy(cp.at[0], prior, sem_alt_p)

    def halo_down(k, buf, c):
        src = cp.at[0, 0, span(c)] if buf is u0 else buf.at[1, padded(c)]
        return pltpu.make_async_remote_copy(
            src, buf.at[top, padded(c)], hs.at[1 - odd], hr.at[k % 2, 0, c],
            device_id={"slab": me_slab - 1}, device_id_type=MESH)

    def halo_up(k, buf, c):
        src = cp.at[0, layers - 1, span(c)] if buf is u0 else buf.at[layers, padded(c)]
        return pltpu.make_async_remote_copy(
            src, buf.at[0, padded(c)], hs.at[odd], hr.at[k % 2, 1, c],
            device_id={"slab": me_slab + 1}, device_id_type=MESH)

    detour = n_slab == 8
    mid = n_slab // 2
    low_mid = me_slab == mid - 1
    high_mid = me_slab == mid

    def goes_round(c):
        return jnp.logical_and(lax.rem(c, 2) == 1, c < CHUNKS - 1)

    def to_relay(k, buf, c, up):
        z = layers if up else 1
        src = cp.at[0, z - 1, span(c)] if buf is u0 else buf.at[z, padded(c)]
        return pltpu.make_async_remote_copy(
            src, passing.at[k, span(c)], hs.at[1], pr.at[k % 2, c // 2],
            device_id={"slab": n_slab - 1 if up else 0}, device_id_type=MESH)

    def from_relay(k, buf, c, up):
        return pltpu.make_async_remote_copy(
            passing.at[k, span(c)], buf.at[0 if up else top, padded(c)],
            hs.at[2], hr.at[k % 2, int(up), c],
            device_id={"slab": mid if up else mid - 1}, device_id_type=MESH)

    def relay(k, buf, c):
        if not detour:
            return

        @pl.when(jnp.logical_and(goes_round(c), jnp.logical_not(has_low)))
        def _():
            to_relay(k, buf, c, False).wait_recv()
            from_relay(k, buf, c, False).start()

        @pl.when(jnp.logical_and(goes_round(c), jnp.logical_not(has_high)))
        def _():
            to_relay(k, buf, c, True).wait_recv()
            from_relay(k, buf, c, True).start()

    far_low = jnp.logical_and(has_low, even)
    far_high = jnp.logical_and(has_high, is_odd)

    def send_close(k, buf, c):
        @pl.when(even)
        def _():
            halo_up(k, buf, c).start()

        @pl.when(is_odd)
        def _():
            halo_down(k, buf, c).start()

    def wait_close(k, buf, c):
        @pl.when(even)
        def _():
            halo_down(k, buf, c).wait_recv()

        @pl.when(is_odd)
        def _():
            halo_up(k, buf, c).wait_recv()

    def send_far(k, buf, c):
        low, high = far_low, far_high
        if detour:
            around = goes_round(c)
            low_round = jnp.logical_and(around, high_mid)
            high_round = jnp.logical_and(around, low_mid)

            @pl.when(low_round)
            def _():
                to_relay(k, buf, c, False).start()

            @pl.when(high_round)
            def _():
                to_relay(k, buf, c, True).start()

            low = jnp.logical_and(low, jnp.logical_not(low_round))
            high = jnp.logical_and(high, jnp.logical_not(high_round))

        @pl.when(low)
        def _():
            halo_down(k, buf, c).start()

        @pl.when(high)
        def _():
            halo_up(k, buf, c).start()

    def wait_far(k, buf, c):
        @pl.when(far_low)
        def _():
            halo_up(k, buf, c).wait_recv()

        @pl.when(far_high)
        def _():
            halo_down(k, buf, c).wait_recv()

    def sent_halos():
        def taken(ref, sem):
            pltpu.make_async_remote_copy(
                ref, ref, sem, hr.at[0, 0, 0],
                device_id={"slab": lax.rem(me_slab + 1, n_slab)}, device_id_type=MESH).wait_send()

        taken(passing, hs.at[0])

        @pl.when(jnp.logical_or(far_low, far_high))
        def _():
            taken(passing, hs.at[1])

        if detour:
            @pl.when(jnp.logical_or(jnp.logical_not(has_low), jnp.logical_not(has_high)))
            def _():
                taken(passing.at[:, pl.ds(0, (CHUNKS - 1) // 2 * size)], hs.at[2])

    rims = (0, layers - 1)

    def back(src, dst, sem):
        return pltpu.make_async_remote_copy(
            src, dst, zs.at[0], sem, device_id={"seg": me_seg - 1}, device_id_type=MESH)

    def onward(at, here, sem):
        return pltpu.make_async_remote_copy(
            end.at[at, here], prior.at[at, here], zs.at[1], sem,
            device_id={"seg": me_seg + 1}, device_id_type=MESH)

    def send_mid(c):
        return back(cp.at[0, mid_at, span(c)], cpn.at[mid_at, span(c)], zr_mid.at[c])

    def half(h):
        return pl.ds(pl.multiple_of(h * (rows // HALVES), 8), rows // HALVES)

    def send_rim(h, j):
        return back(cp.at[0, rims[j], half(h)], cpn.at[rims[j], half(h)], zr_rim.at[h])

    def both_rims(h):
        two = pl.ds(0, 2)
        return back(cp.at[0, two, half(h)], cpn.at[two, half(h)], zr_rim.at[h])

    def send_next(q):
        here = pl.ds(pl.multiple_of(q * (rows // QUARTERS), 8), rows // QUARTERS)
        return back(cp.at[0, next_at, here], cpn.at[next_at, here], zr_next.at[q])

    def send_far_end(c):
        return onward(far_at, span(c), zr_end.at[c])

    def send_near_end(at, r, count):
        return onward(at, pl.ds(pl.multiple_of(r, 8), count), zr_near)

    def all_near_ends():
        return onward(near_at, pl.ds(0, rows), zr_near)

    barrier = pltpu.get_barrier_semaphore()
    slab_peers = [{"slab": lax.rem(me_slab + d, n_slab)} for d in range(1, n_slab)]
    seg_peers = [{"seg": lax.rem(me_seg + d, n_seg)} for d in range(1, n_seg)]
    both = [
        {"seg": lax.rem(me_seg + e, n_seg), "slab": lax.rem(me_slab + d, n_slab)}
        for e in range(1, n_seg) for d in range(1, n_slab)
    ]
    direct = n_seg * n_slab <= 32
    near = slab_peers + seg_peers
    peers = near + both
    for peer in near:
        pl.semaphore_signal(barrier, inc=1, device_id=peer, device_id_type=MESH)

    for copy in loads(0):
        copy.start()

    pl.semaphore_wait(barrier, len(near))

    send_first(0)

    @pl.when(jnp.logical_not(first))
    def _():
        for j in range(2):
            send_rim(0, j).start()

    send_far(0, u0, 0)
    for copy in loads(1):
        copy.start()
    send_first(1)

    edge = jnp.zeros((PAD, cols), jnp.float32)
    for buf in (u0, u1, l2, l1):
        for z in range(1, top):
            buf[z, pl.ds(0, PAD), :] = edge
            buf[z, pl.ds(rows + PAD, PAD), :] = edge

    def clear(z):
        @pl.loop(0, rows // PAD)
        def _(i):
            for buf in (u0, u1, l2, l1):
                buf[z, pl.ds(pl.multiple_of(i * PAD + PAD, 8), PAD), :] = edge

    @pl.when(jnp.logical_not(has_low))
    def _():
        clear(0)

    @pl.when(jnp.logical_not(has_high))
    def _():
        clear(top)

    acc[...] = jnp.zeros_like(acc)

    lane = lax.broadcasted_iota(jnp.int32, (TILE, cols), 1)
    at_left = lane == 0
    at_right = lane == cols - 1

    def laplace(buf, z, r):
        tall = buf[z, pl.ds(pl.multiple_of(r - PAD, 8), TILE + 2 * PAD), :]
        mid = tall[PAD:PAD + TILE]
        beside = buf[z + 1, pl.ds(r, TILE), :] + buf[z - 1, pl.ds(r, TILE), :]
        beside = beside + (tall[PAD + 1:PAD + 1 + TILE] + tall[PAD - 1:PAD - 1 + TILE])
        right = jnp.where(at_right, 0.0, pltpu.roll(mid, cols - 1, 1))
        left = jnp.where(at_left, 0.0, pltpu.roll(mid, 1, 1))
        return mid, beside + (right + left) - 6.0 * mid

    def each_tile(c, body, zs, shift=0, count=tiles):
        def at_tile(i):
            r = pl.multiple_of(c * size + shift + i * TILE, 8)
            for z in zs:
                body(z, r, pl.ds(r, TILE), pl.multiple_of(r + PAD, 8))

        if len(zs) > 2:
            pl.loop(0, count)(at_tile)
        else:
            for i in range(count):
                at_tile(i)

    def add_square(v):
        sq = v * v
        part = sq[:PAD]
        for i in range(1, TILE // PAD):
            part = part + sq[i * PAD:(i + 1) * PAD]
        acc[...] = acc[...] + part

    def forward(src, c, dst, zs, shift=0, count=tiles):
        def body(z, r, at, p):
            u, lap = laplace(src, z + 1, p)
            new = u + 0.1 * (lap + rat[z, at, :] * u * (1.0 - u) + ctl[z, at, :])
            if dst is u1:
                u1[z + 1, pl.ds(p, TILE), :] = new
            else:
                end[z, at, :] = new
        each_tile(c, body, zs, shift, count)

    def between(i, low, high):
        return pl.when(jnp.logical_and(i >= low, i < high))

    @pl.loop(0, CHUNKS + LAG_U)
    def _(i):
        for j, step in enumerate((0, 1, 3)):
            @pl.when(i == step)
            def _():
                for copy in loads(j):
                    copy.wait()
                wait_first(j)

        @pl.when(i < CHUNKS)
        def _():
            forward(u0, i, u1, [close, *mids, next_far])
            send_close(1, u1, i)

        def do_mids(shift, count):
            forward(u1, i, end, mids, shift, count)

            @pl.when(jnp.logical_not(last))
            def _():
                send_near_end(mid_at, i * size + shift, count * TILE).start()

        @pl.when(i == 0)
        def _():
            do_mids(0, 1)
            for copy in loads(2):
                copy.start()
            send_first(2)

            @pl.loop(1, CHUNKS)
            def _(c):
                send_far(0, u0, c)

        @between(i, 1, CHUNKS)
        def _():
            do_mids(TILE - size, tiles)

        @pl.when(i == CHUNKS)
        def _():
            do_mids(TILE - size, tiles - 1)

        @pl.when(i == 1)
        def _():
            if direct:
                for peer in slab_peers:
                    pl.semaphore_signal(ready, inc=1, device_id=peer, device_id_type=MESH)

            @pl.when(last)
            def _():
                alt_c().start()

            @pl.when(first)
            def _():
                alt_p().start()

        @between(i, 2, CHUNKS + 2)
        def _():
            c = i - 2
            wait_close(1, u1, c)
            forward(u1, c, end, [close])

            @pl.when(jnp.logical_not(last))
            def _():
                send_near_end(close_at, c * size, size).start()

        @pl.when(jnp.logical_not(first))
        def _():
            for h in range(1, HALVES):
                @pl.when(i == h)
                def _():
                    for j in range(2):
                        send_rim(h, j).start()

            @between(i, HALVES, HALVES + QUARTERS)
            def _():
                send_next(i - HALVES).start()

            @pl.when(i >= LAG_U)
            def _():
                send_mid(i - LAG_U).start()

        @between(i, LAG_B - 1, CHUNKS + LAG_B - 1)
        def _():
            relay(0, u0, i - LAG_B + 1)

        @between(i, LAG_B, CHUNKS + LAG_B)
        def _():
            c = i - LAG_B
            wait_far(0, u0, c)
            forward(u0, c, u1, [far])
            send_far(1, u1, c)

        @between(i, LAG_B + 2, CHUNKS + LAG_B + 2)
        def _():
            relay(1, u1, i - LAG_B - 2)

        @pl.when(i >= LAG_U)
        def _():
            c = i - LAG_U
            wait_far(1, u1, c)
            forward(u1, c, end, [next_far, far])

            @pl.when(jnp.logical_not(last))
            def _():
                send_far_end(c).start()

    def defect(c, zs):
        def body(z, r, at, p):
            l2[z + 1, pl.ds(p, TILE), :] = end[z, at, :] - cpn[z, at, :]
        each_tile(c, body, zs)

    @pl.when(last)
    def _():
        alt_c().wait()

    @pl.when(first)
    def _():
        alt_p().wait()

    @pl.loop(0, CHUNKS)
    def _(c):
        @pl.when(jnp.logical_and(jnp.logical_not(last), lax.rem(c, CHUNKS // HALVES) == 0))
        def _():
            both_rims(c // (CHUNKS // HALVES)).wait_recv()
        defect(c, rims)
        send_far(2, l2, c)
        send_close(2, l2, c)

    def do_l1(c, zs):
        def body(z, r, at, p):
            lam, lap = laplace(l2, z + 1, p)
            new = lam + 0.1 * (lap + rat[z, at, :] * (1.0 - 2.0 * u1[z + 1, pl.ds(p, TILE), :]) * lam)
            l1[z + 1, pl.ds(p, TILE), :] = new
            g = 0.1 * (lam + new)
            gc[z, at, :] = g
            add_square(g)
        each_tile(c, body, zs)

    def do_l0(c, zs, whole=False):
        def body(z, r, at, p):
            lam, lap = laplace(l1, z + 1, p)
            start = u0[z + 1, pl.ds(p, TILE), :]
            g = lam + 0.1 * (lap + rat[z, at, :] * (1.0 - 2.0 * start) * lam)
            if whole:
                g = g - (prior[z, at, :] - start)
                add_square(g)
            gs[z, at, :] = g
        each_tile(c, body, zs)

    def do_start(c):
        @pl.when(jnp.logical_not(first))
        def _():
            send_far_end(c).wait_recv()

        def body(z, r, at, p):
            g = gs[z, at, :] - (prior[z, at, :] - u0[z + 1, pl.ds(p, TILE), :])
            gs[z, at, :] = g
            add_square(g)
        each_tile(c, body, [next_far, far])

    relay(2, l2, 1)

    @pl.loop(0, CHUNKS)
    def _(c):
        @pl.when(jnp.logical_and(jnp.logical_not(last), lax.rem(c, CHUNKS // QUARTERS) == 0))
        def _():
            send_next(c // (CHUNKS // QUARTERS)).wait_recv()
        defect(c, [next_far])

        @pl.when(c < CHUNKS - 2)
        def _():
            relay(2, l2, c + 2)
        wait_far(2, l2, c)
        do_l1(c, [far])
        send_far(3, l1, c)

        @pl.when(c >= 1)
        def _():
            relay(3, l1, c - 1)

    @pl.when(jnp.logical_not(first))
    def _():
        all_near_ends().wait_recv()

    @pl.loop(0, CHUNKS + LAG_0)
    def _(i):
        @pl.when(i < CHUNKS)
        def _():
            @pl.when(jnp.logical_not(last))
            def _():
                send_mid(i).wait_recv()
            defect(i, mids)
            wait_close(2, l2, i)
            do_l1(i, [close, next_far])
            send_close(3, l1, i)

        @between(i, 1, CHUNKS + 1)
        def _():
            do_l1(i - 1, mids)

        @pl.when(i < CHUNKS)
        def _():
            wait_far(3, l1, i)
            do_l0(i, [far])

        @between(i, 1, CHUNKS + 1)
        def _():
            do_l0(i - 1, [next_far])

        @pl.when(i >= LAG_0)
        def _():
            c = i - LAG_0
            wait_close(3, l1, c)
            do_l0(c, [close, *mids], True)
            do_start(c)

    def sent_all():
        sent_halos()

        @pl.when(jnp.logical_not(first))
        def _():
            back(cp.at[0], cpn, zr_mid.at[0]).wait_send()

        @pl.when(jnp.logical_not(last))
        def _():
            onward(pl.ds(0, layers), pl.ds(0, rows), zr_end.at[0]).wait_send()

    tile = acc[:, :128]
    for j in range(1, cols // 128):
        tile = tile + acc[:, j * 128:(j + 1) * 128]
    tile = jnp.sum(tile, axis=0, keepdims=True)

    def total(value, slots, owner, peers, ss, sr):
        count = len(peers)

        def copy(at, peer):
            return pltpu.make_async_remote_copy(
                slots.at[at], slots.at[at], ss, sr, device_id=peer, device_id_type=MESH)

        slots[owner] = value
        for peer in peers:
            copy(owner, peer).start()
        if slots is slot_a:
            sent_all()
        everything = copy(pl.ds(0, count), peers[0])
        everything.wait_recv()
        result = slots[0]
        for j in range(1, count + 1):
            result = result + slots[j]
        return result, everything

    if direct:
        pl.semaphore_wait(ready, len(slab_peers))
        tile, sent_a = total(tile, slot_a, me_seg * n_slab + me_slab, peers, as_, ar)
        sent = [sent_a]
    else:
        tile, sent_a = total(tile, slot_a, me_slab, slab_peers, as_, ar)
        tile, sent_b = total(tile, slot_b, me_seg, seg_peers, bs, br)
        sent = [sent_a, sent_b]
    tot_out[...] = tile
    for copies in sent:
        copies.wait_send()


def update_kernel(
    count, u0, ctl, gs, gc, tot, new_cp, new_ctl, out_a, out_b, sem_a, sem_b
):
    layers, rows, cols = ctl.shape
    size = rows // PARTS
    sum_of = jnp.sum(tot[...], axis=1, keepdims=True)
    scale = jnp.broadcast_to(0.5 / jnp.sqrt(sum_of / count + 1e-06), (PAD, cols))

    def save(c):
        at = pl.ds(pl.multiple_of(c * size, size), size)
        return (
            pltpu.make_async_copy(out_a.at[:, at], new_cp.at[0, :, at], sem_a),
            pltpu.make_async_copy(out_b.at[:, at], new_ctl.at[0, :, at], sem_b),
        )

    @pl.loop(0, PARTS)
    def _(c):
        @pl.loop(0, size // PAD)
        def _(i):
            r = pl.multiple_of(c * size + i * PAD, 8)
            at = pl.ds(r, PAD)
            for z in range(layers):
                start = u0[z + 1, pl.ds(pl.multiple_of(r + PAD, 8), PAD), :]
                out_a[z, at, :] = start - scale * gs[z, at, :]
                out_b[z, at, :] = ctl[z, at, :] - scale * gc[z, at, :]
        for copy in save(c):
            copy.start()

    pltpu.make_async_copy(out_a, new_cp.at[0], sem_a).wait()
    pltpu.make_async_copy(out_b, new_ctl.at[0], sem_b).wait()


def per_device(checkpoints, control, rate, target):
    n_seg = lax.axis_size("seg")
    n_slab = lax.axis_size("slab")
    layers, rows, cols = rate.shape
    f32 = jnp.float32
    block = pltpu.VMEM((layers, rows, cols), f32)
    wide = pltpu.VMEM((layers + 2, rows + 2 * PAD, cols), f32)
    dma = pltpu.SemaphoreType.DMA
    hbm = pl.BlockSpec(memory_space=pltpu.HBM)
    vmem = pl.BlockSpec(memory_space=pltpu.VMEM)
    kept = pl.pallas_call(
        functools.partial(kernel, n_seg, n_slab),
        out_shape=(wide, block, block, block, pltpu.VMEM((1, 128), f32)),
        in_specs=[hbm] * 4,
        out_specs=(vmem,) * 5,
        scratch_shapes=[
            wide, wide, wide,
            block, block, block, block,
            pltpu.VMEM((PAD, cols), f32),
            pltpu.VMEM((n_slab * n_seg, 1, 128), f32),
            pltpu.VMEM((n_seg, 1, 128), f32),
            dma((3,)), dma((3,)), dma((3,)),
            dma(()), dma(()),
            dma((3,)), dma((2, 2, CHUNKS)),
            dma((2,)), dma((CHUNKS,)), dma(()), dma((CHUNKS,)), dma((HALVES,)), dma((QUARTERS,)),
            dma(()), dma(()), dma(()), dma(()),
            pltpu.VMEM((4, rows, cols), f32), dma((2, CHUNKS // 2)),
            pltpu.SemaphoreType.REGULAR,
        ],
        compiler_params=pltpu.CompilerParams(
            collective_id=0, has_side_effects=True, vmem_limit_bytes=50 << 20
        ),
        name="shooting",
    )(checkpoints, control, rate, target)
    count = 2.0 * n_seg * n_slab * rate.size
    return pl.pallas_call(
        functools.partial(update_kernel, count),
        out_shape=(
            jax.ShapeDtypeStruct(checkpoints.shape, f32),
            jax.ShapeDtypeStruct(control.shape, f32),
        ),
        in_specs=[vmem] * 5,
        out_specs=(hbm, hbm),
        scratch_shapes=[block, block, dma(()), dma(())],
        compiler_params=pltpu.CompilerParams(vmem_limit_bytes=8 << 20),
        name="update",
    )(*kept)


def solution(mesh):
    return jax.shard_map(
        per_device,
        mesh=mesh,
        in_specs=(
            P("seg", "slab", None, None),
            P("seg", "slab", None, None),
            P("slab", None, None),
            P("slab", None, None),
        ),
        out_specs=(P("seg", "slab", None, None), P("seg", "slab", None, None)),
        check_vma=False,
    )
```

```python
import functools

import jax
import jax.numpy as jnp
from jax import lax
from jax.experimental import pallas as pl
from jax.experimental.pallas import tpu as pltpu
from jax.sharding import PartitionSpec as P

CHUNKS = 8
PARTS = 8
TILE = 16
PAD = 8
LAG_B = 2
LAG_U = 6
HALVES = 2
QUARTERS = 4
LAG_0 = 2
MESH = pl.DeviceIdType.MESH


def kernel(
    n_seg, n_slab,
    cp, ctl_in, rate_in, target,
    u0, ctl, gs, gc, tot_out,
    u1, l2, l1, rat, end, cpn, prior, acc, slot_a, slot_b,
    sem_u0, sem_ctl, sem_rat, sem_alt_c, sem_alt_p,
    hs, hr_first, hr_close, hr_far, zs, zr_end, zr_near, zr_mid, zr_rim, zr_next, as_, ar, bs, br,
    ready,
):
    me_seg = lax.axis_index("seg")
    me_slab = lax.axis_index("slab")
    layers, rows, cols = cp.shape[1:]
    size = rows // CHUNKS
    tiles = size // TILE
    top = layers + 1
    has_low = me_slab > 0
    has_high = me_slab < n_slab - 1
    first = me_seg == 0
    last = me_seg == n_seg - 1

    def span(c):
        return pl.ds(pl.multiple_of(c * size, size), size)

    def padded(c):
        return pl.ds(pl.multiple_of(c * size + PAD, 8), size)

    odd = lax.rem(me_slab, 2)

    def layer(j):
        return (1 - odd) * (layers - 1 - j) + odd * j

    close = layer(0)
    mids = [layer(j) for j in range(1, layers - 2)]
    next_far = layer(layers - 2)
    far = layer(layers - 1)
    mid_at = pl.ds(2 - odd, layers - 3)
    next_at = pl.ds(next_far, 1)
    close_at = pl.ds(close, 1)
    far_at = pl.ds(odd * (layers - 2), 2)

    near_at = pl.ds(2 * (1 - odd), layers - 2)

    begin = size + PAD
    later = min(begin + 2 * size, rows)
    pieces = ((0, begin), (begin, later - begin), (later, rows - later))

    def loads(j):
        at, count = pieces[j]
        here = pl.ds(at, count)
        return (
            pltpu.make_async_copy(
                cp.at[0, :, here], u0.at[pl.ds(1, layers), pl.ds(at + PAD, count)], sem_u0.at[j % 2]),
            pltpu.make_async_copy(ctl_in.at[0, :, here], ctl.at[:, here], sem_ctl.at[j % 2]),
            pltpu.make_async_copy(rate_in.at[:, here], rat.at[:, here], sem_rat.at[j % 2]),
        )

    has_far = jnp.logical_or(
        jnp.logical_and(has_low, odd == 0), jnp.logical_and(has_high, odd == 1))
    partner = {"slab": me_slab + 1 - 2 * odd}
    beyond = {"slab": me_slab - 1 + 2 * odd}

    def first_halo(j):
        at, count = pieces[j]
        return pltpu.make_async_remote_copy(
            cp.at[0, close, pl.ds(at, count)], u0.at[odd * top, pl.ds(at + PAD, count)],
            hs.at[0], hr_first.at[j], device_id=partner, device_id_type=MESH)

    def close_halo(k, buf, c):
        return pltpu.make_async_remote_copy(
            buf.at[close + 1, padded(c)], buf.at[odd * top, padded(c)],
            hs.at[0], hr_close.at[k % 2, c], device_id=partner, device_id_type=MESH)

    def far_halo(k, buf, c):
        src = cp.at[0, far, span(c)] if buf is u0 else buf.at[far + 1, padded(c)]
        return pltpu.make_async_remote_copy(
            src, buf.at[(1 - odd) * top, padded(c)],
            hs.at[1], hr_far.at[k % 2, c], device_id=beyond, device_id_type=MESH)

    def send_first(j):
        first_halo(j).start()

    def wait_first(j):
        first_halo(j).wait_recv()

    def send_close(k, buf, c):
        close_halo(k, buf, c).start()

    def wait_close(k, buf, c):
        close_halo(k, buf, c).wait_recv()

    def send_far(k, buf, c):
        @pl.when(has_far)
        def _():
            far_halo(k, buf, c).start()

    def wait_far(k, buf, c):
        @pl.when(has_far)
        def _():
            far_halo(k, buf, c).wait_recv()

    def alt_c():
        return pltpu.make_async_copy(target, cpn, sem_alt_c)

    def alt_p():
        return pltpu.make_async_copy(cp.at[0], prior, sem_alt_p)

    def sent_halos():
        def taken(sem):
            four = u1.at[pl.ds(0, 4), pl.ds(0, rows)]
            pltpu.make_async_remote_copy(
                four, four, sem, hr_first.at[0],
                device_id=partner, device_id_type=MESH).wait_send()

        taken(hs.at[0])

        @pl.when(has_far)
        def _():
            taken(hs.at[1])

    rims = (0, layers - 1)

    def back(src, dst, sem):
        return pltpu.make_async_remote_copy(
            src, dst, zs.at[0], sem, device_id={"seg": me_seg - 1}, device_id_type=MESH)

    def onward(at, here, sem):
        return pltpu.make_async_remote_copy(
            end.at[at, here], prior.at[at, here], zs.at[1], sem,
            device_id={"seg": me_seg + 1}, device_id_type=MESH)

    def send_mid(c):
        return back(cp.at[0, mid_at, span(c)], cpn.at[mid_at, span(c)], zr_mid.at[c])

    def half(h):
        return pl.ds(pl.multiple_of(h * (rows // HALVES), 8), rows // HALVES)

    def send_rim(h, j):
        return back(cp.at[0, rims[j], half(h)], cpn.at[rims[j], half(h)], zr_rim.at[h])

    def both_rims(h):
        two = pl.ds(0, 2)
        return back(cp.at[0, two, half(h)], cpn.at[two, half(h)], zr_rim.at[h])

    def send_next(q):
        here = pl.ds(pl.multiple_of(q * (rows // QUARTERS), 8), rows // QUARTERS)
        return back(cp.at[0, next_at, here], cpn.at[next_at, here], zr_next.at[q])

    def send_far_end(c):
        return onward(far_at, span(c), zr_end.at[c])

    def send_near_end(at, r, count):
        return onward(at, pl.ds(pl.multiple_of(r, 8), count), zr_near)

    def all_near_ends():
        return onward(near_at, pl.ds(0, rows), zr_near)

    barrier = pltpu.get_barrier_semaphore()
    slab_peers = [{"slab": lax.rem(me_slab + d, n_slab)} for d in range(1, n_slab)]
    seg_peers = [{"seg": lax.rem(me_seg + d, n_seg)} for d in range(1, n_seg)]
    both = [
        {"seg": lax.rem(me_seg + e, n_seg), "slab": lax.rem(me_slab + d, n_slab)}
        for e in range(1, n_seg) for d in range(1, n_slab)
    ]
    direct = n_seg * n_slab <= 32
    near = slab_peers + seg_peers
    peers = near + both
    for peer in near:
        pl.semaphore_signal(barrier, inc=1, device_id=peer, device_id_type=MESH)

    for copy in loads(0):
        copy.start()

    pl.semaphore_wait(barrier, len(near))

    send_first(0)

    @pl.when(jnp.logical_not(first))
    def _():
        for j in range(2):
            send_rim(0, j).start()

    send_far(0, u0, 0)
    for copy in loads(1):
        copy.start()
    send_first(1)

    edge = jnp.zeros((PAD, cols), jnp.float32)
    for buf in (u0, u1, l2, l1):
        for z in range(1, top):
            buf[z, pl.ds(0, PAD), :] = edge
            buf[z, pl.ds(rows + PAD, PAD), :] = edge

    def clear(z):
        @pl.loop(0, rows // PAD)
        def _(i):
            for buf in (u0, u1, l2, l1):
                buf[z, pl.ds(pl.multiple_of(i * PAD + PAD, 8), PAD), :] = edge

    @pl.when(jnp.logical_not(has_low))
    def _():
        clear(0)

    @pl.when(jnp.logical_not(has_high))
    def _():
        clear(top)

    acc[...] = jnp.zeros_like(acc)

    lane = lax.broadcasted_iota(jnp.int32, (TILE, cols), 1)
    at_left = lane == 0
    at_right = lane == cols - 1

    def laplace(buf, z, r):
        tall = buf[z, pl.ds(pl.multiple_of(r - PAD, 8), TILE + 2 * PAD), :]
        mid = tall[PAD:PAD + TILE]
        beside = buf[z + 1, pl.ds(r, TILE), :] + buf[z - 1, pl.ds(r, TILE), :]
        beside = beside + (tall[PAD + 1:PAD + 1 + TILE] + tall[PAD - 1:PAD - 1 + TILE])
        right = jnp.where(at_right, 0.0, pltpu.roll(mid, cols - 1, 1))
        left = jnp.where(at_left, 0.0, pltpu.roll(mid, 1, 1))
        return mid, beside + (right + left) - 6.0 * mid

    def each_tile(c, body, zs, shift=0, count=tiles):
        def at_tile(i):
            r = pl.multiple_of(c * size + shift + i * TILE, 8)
            for z in zs:
                body(z, r, pl.ds(r, TILE), pl.multiple_of(r + PAD, 8))

        if len(zs) > 2:
            pl.loop(0, count)(at_tile)
        else:
            for i in range(count):
                at_tile(i)

    def add_square(v):
        sq = v * v
        part = sq[:PAD]
        for i in range(1, TILE // PAD):
            part = part + sq[i * PAD:(i + 1) * PAD]
        acc[...] = acc[...] + part

    def forward(src, c, dst, zs, shift=0, count=tiles):
        def body(z, r, at, p):
            u, lap = laplace(src, z + 1, p)
            new = u + 0.1 * (lap + rat[z, at, :] * u * (1.0 - u) + ctl[z, at, :])
            if dst is u1:
                u1[z + 1, pl.ds(p, TILE), :] = new
            else:
                end[z, at, :] = new
        each_tile(c, body, zs, shift, count)

    def between(i, low, high):
        return pl.when(jnp.logical_and(i >= low, i < high))

    @pl.loop(0, CHUNKS + LAG_U)
    def _(i):
        for j, step in enumerate((0, 1, 3)):
            @pl.when(i == step)
            def _():
                for copy in loads(j):
                    copy.wait()
                wait_first(j)

        @pl.when(i < CHUNKS)
        def _():
            forward(u0, i, u1, [close, *mids, next_far])
            send_close(1, u1, i)

        def do_mids(shift, count):
            forward(u1, i, end, mids, shift, count)

            @pl.when(jnp.logical_not(last))
            def _():
                send_near_end(mid_at, i * size + shift, count * TILE).start()

        @pl.when(i == 0)
        def _():
            do_mids(0, 1)
            for copy in loads(2):
                copy.start()
            send_first(2)

            @pl.loop(1, CHUNKS)
            def _(c):
                send_far(0, u0, c)

        @between(i, 1, CHUNKS)
        def _():
            do_mids(TILE - size, tiles)

        @pl.when(i == CHUNKS)
        def _():
            do_mids(TILE - size, tiles - 1)

        @pl.when(i == 1)
        def _():
            if direct:
                for peer in slab_peers:
                    pl.semaphore_signal(ready, inc=1, device_id=peer, device_id_type=MESH)

            @pl.when(last)
            def _():
                alt_c().start()

            @pl.when(first)
            def _():
                alt_p().start()

        @between(i, 2, CHUNKS + 2)
        def _():
            c = i - 2
            wait_close(1, u1, c)
            forward(u1, c, end, [close])

            @pl.when(jnp.logical_not(last))
            def _():
                send_near_end(close_at, c * size, size).start()

        @pl.when(jnp.logical_not(first))
        def _():
            for h in range(1, HALVES):
                @pl.when(i == h)
                def _():
                    for j in range(2):
                        send_rim(h, j).start()

            @between(i, HALVES, HALVES + QUARTERS)
            def _():
                send_next(i - HALVES).start()

            @pl.when(i >= LAG_U)
            def _():
                send_mid(i - LAG_U).start()

        @between(i, LAG_B, CHUNKS + LAG_B)
        def _():
            c = i - LAG_B
            wait_far(0, u0, c)
            forward(u0, c, u1, [far])
            send_far(1, u1, c)

        @pl.when(i >= LAG_U)
        def _():
            c = i - LAG_U
            wait_far(1, u1, c)
            forward(u1, c, end, [next_far, far])

            @pl.when(jnp.logical_not(last))
            def _():
                send_far_end(c).start()

    def defect(c, zs):
        def body(z, r, at, p):
            l2[z + 1, pl.ds(p, TILE), :] = end[z, at, :] - cpn[z, at, :]
        each_tile(c, body, zs)

    @pl.when(last)
    def _():
        alt_c().wait()

    @pl.when(first)
    def _():
        alt_p().wait()

    @pl.loop(0, CHUNKS)
    def _(c):
        @pl.when(jnp.logical_and(jnp.logical_not(last), lax.rem(c, CHUNKS // HALVES) == 0))
        def _():
            both_rims(c // (CHUNKS // HALVES)).wait_recv()
        defect(c, rims)
        send_far(2, l2, c)
        send_close(2, l2, c)

    def do_l1(c, zs):
        def body(z, r, at, p):
            lam, lap = laplace(l2, z + 1, p)
            new = lam + 0.1 * (lap + rat[z, at, :] * (1.0 - 2.0 * u1[z + 1, pl.ds(p, TILE), :]) * lam)
            l1[z + 1, pl.ds(p, TILE), :] = new
            g = 0.1 * (lam + new)
            gc[z, at, :] = g
            add_square(g)
        each_tile(c, body, zs)

    def do_l0(c, zs, whole=False):
        def body(z, r, at, p):
            lam, lap = laplace(l1, z + 1, p)
            start = u0[z + 1, pl.ds(p, TILE), :]
            g = lam + 0.1 * (lap + rat[z, at, :] * (1.0 - 2.0 * start) * lam)
            if whole:
                g = g - (prior[z, at, :] - start)
                add_square(g)
            gs[z, at, :] = g
        each_tile(c, body, zs)

    def do_start(c):
        @pl.when(jnp.logical_not(first))
        def _():
            send_far_end(c).wait_recv()

        def body(z, r, at, p):
            g = gs[z, at, :] - (prior[z, at, :] - u0[z + 1, pl.ds(p, TILE), :])
            gs[z, at, :] = g
            add_square(g)
        each_tile(c, body, [next_far, far])

    @pl.loop(0, CHUNKS)
    def _(c):
        @pl.when(jnp.logical_and(jnp.logical_not(last), lax.rem(c, CHUNKS // QUARTERS) == 0))
        def _():
            send_next(c // (CHUNKS // QUARTERS)).wait_recv()
        defect(c, [next_far])

        wait_far(2, l2, c)
        do_l1(c, [far])
        send_far(3, l1, c)

    @pl.when(jnp.logical_not(first))
    def _():
        all_near_ends().wait_recv()

    @pl.loop(0, CHUNKS + LAG_0)
    def _(i):
        @pl.when(i < CHUNKS)
        def _():
            @pl.when(jnp.logical_not(last))
            def _():
                send_mid(i).wait_recv()
            defect(i, mids)
            wait_close(2, l2, i)
            do_l1(i, [close, next_far])
            send_close(3, l1, i)

        @between(i, 1, CHUNKS + 1)
        def _():
            do_l1(i - 1, mids)

        @pl.when(i < CHUNKS)
        def _():
            wait_far(3, l1, i)
            do_l0(i, [far])

        @between(i, 1, CHUNKS + 1)
        def _():
            do_l0(i - 1, [next_far])

        @pl.when(i >= LAG_0)
        def _():
            c = i - LAG_0
            wait_close(3, l1, c)
            do_l0(c, [close, *mids], True)
            do_start(c)

    def sent_all():
        sent_halos()

        @pl.when(jnp.logical_not(first))
        def _():
            back(cp.at[0], cpn, zr_mid.at[0]).wait_send()

        @pl.when(jnp.logical_not(last))
        def _():
            onward(pl.ds(0, layers), pl.ds(0, rows), zr_end.at[0]).wait_send()

    tile = acc[:, :128]
    for j in range(1, cols // 128):
        tile = tile + acc[:, j * 128:(j + 1) * 128]
    tile = jnp.sum(tile, axis=0, keepdims=True)

    def total(value, slots, owner, peers, ss, sr):
        count = len(peers)

        def copy(at, peer):
            return pltpu.make_async_remote_copy(
                slots.at[at], slots.at[at], ss, sr, device_id=peer, device_id_type=MESH)

        slots[owner] = value
        for peer in peers:
            copy(owner, peer).start()
        if slots is slot_a:
            sent_all()
        everything = copy(pl.ds(0, count), peers[0])
        everything.wait_recv()
        result = slots[0]
        for j in range(1, count + 1):
            result = result + slots[j]
        return result, everything

    if direct:
        pl.semaphore_wait(ready, len(slab_peers))
        tile, sent_a = total(tile, slot_a, me_seg * n_slab + me_slab, peers, as_, ar)
        sent = [sent_a]
    else:
        tile, sent_a = total(tile, slot_a, me_slab, slab_peers, as_, ar)
        tile, sent_b = total(tile, slot_b, me_seg, seg_peers, bs, br)
        sent = [sent_a, sent_b]
    tot_out[...] = tile
    for copies in sent:
        copies.wait_send()


def update_kernel(
    count, u0, ctl, gs, gc, tot, new_cp, new_ctl, out_a, out_b, sem_a, sem_b
):
    layers, rows, cols = ctl.shape
    size = rows // PARTS
    sum_of = jnp.sum(tot[...], axis=1, keepdims=True)
    scale = jnp.broadcast_to(0.5 / jnp.sqrt(sum_of / count + 1e-06), (PAD, cols))

    def save(c):
        at = pl.ds(pl.multiple_of(c * size, size), size)
        return (
            pltpu.make_async_copy(out_a.at[:, at], new_cp.at[0, :, at], sem_a),
            pltpu.make_async_copy(out_b.at[:, at], new_ctl.at[0, :, at], sem_b),
        )

    @pl.loop(0, PARTS)
    def _(c):
        @pl.loop(0, size // PAD)
        def _(i):
            r = pl.multiple_of(c * size + i * PAD, 8)
            at = pl.ds(r, PAD)
            for z in range(layers):
                start = u0[z + 1, pl.ds(pl.multiple_of(r + PAD, 8), PAD), :]
                out_a[z, at, :] = start - scale * gs[z, at, :]
                out_b[z, at, :] = ctl[z, at, :] - scale * gc[z, at, :]
        for copy in save(c):
            copy.start()

    pltpu.make_async_copy(out_a, new_cp.at[0], sem_a).wait()
    pltpu.make_async_copy(out_b, new_ctl.at[0], sem_b).wait()


def per_device(checkpoints, control, rate, target):
    n_seg = lax.axis_size("seg")
    n_slab = lax.axis_size("slab")
    layers, rows, cols = rate.shape
    f32 = jnp.float32
    block = pltpu.VMEM((layers, rows, cols), f32)
    wide = pltpu.VMEM((layers + 2, rows + 2 * PAD, cols), f32)
    dma = pltpu.SemaphoreType.DMA
    hbm = pl.BlockSpec(memory_space=pltpu.HBM)
    vmem = pl.BlockSpec(memory_space=pltpu.VMEM)
    kept = pl.pallas_call(
        functools.partial(kernel, n_seg, n_slab),
        out_shape=(wide, block, block, block, pltpu.VMEM((1, 128), f32)),
        in_specs=[hbm] * 4,
        out_specs=(vmem,) * 5,
        scratch_shapes=[
            wide, wide, wide,
            block, block, block, block,
            pltpu.VMEM((PAD, cols), f32),
            pltpu.VMEM((n_slab * n_seg, 1, 128), f32),
            pltpu.VMEM((n_seg, 1, 128), f32),
            dma((2,)), dma((2,)), dma((2,)),
            dma(()), dma(()),
            dma((2,)), dma((3,)), dma((2, CHUNKS)), dma((2, CHUNKS)),
            dma((2,)), dma((CHUNKS,)), dma(()), dma((CHUNKS,)), dma((HALVES,)), dma((QUARTERS,)),
            dma(()), dma(()), dma(()), dma(()),
            pltpu.SemaphoreType.REGULAR,
        ],
        compiler_params=pltpu.CompilerParams(
            collective_id=0, has_side_effects=True, vmem_limit_bytes=50 << 20
        ),
        name="shooting",
    )(checkpoints, control, rate, target)
    count = 2.0 * n_seg * n_slab * rate.size
    return pl.pallas_call(
        functools.partial(update_kernel, count),
        out_shape=(
            jax.ShapeDtypeStruct(checkpoints.shape, f32),
            jax.ShapeDtypeStruct(control.shape, f32),
        ),
        in_specs=[vmem] * 5,
        out_specs=(hbm, hbm),
        scratch_shapes=[block, block, dma(()), dma(())],
        compiler_params=pltpu.CompilerParams(vmem_limit_bytes=8 << 20),
        name="update",
    )(*kept)


def solution(mesh):
    return jax.shard_map(
        per_device,
        mesh=mesh,
        in_specs=(
            P("seg", "slab", None, None),
            P("seg", "slab", None, None),
            P("slab", None, None),
            P("slab", None, None),
        ),
        out_specs=(P("seg", "slab", None, None), P("seg", "slab", None, None)),
        check_vma=False,
    )
```

```python
import functools

import jax
import jax.numpy as jnp
from jax import lax
from jax.experimental import pallas as pl
from jax.experimental.pallas import tpu as pltpu
from jax.sharding import PartitionSpec as P

CHUNKS = 8
PARTS = 8
TILE = 16
PAD = 8
LAG_B = 2
LAG_U = 6
HALVES = 2
QUARTERS = 4
LAG_0 = 2
MESH = pl.DeviceIdType.MESH


def kernel(
    n_seg, n_slab,
    cp, ctl_in, rate_in, target,
    u0, ctl, gs, gc, tot_out,
    u1, l2, l1, rat, end, cpn, prior, acc, slot_a, slot_b,
    sem_u0, sem_ctl, sem_rat, sem_alt,
    hs, hr_first, hr_close, hr_far, zs, zr_end, zr_near, zr_mid, zr_rim, zr_next, as_, ar, bs, br,
    ready,
):
    me_seg = lax.axis_index("seg")
    me_slab = lax.axis_index("slab")
    layers, rows, cols = cp.shape[1:]
    size = rows // CHUNKS
    tiles = size // TILE
    top = layers + 1
    has_low = me_slab > 0
    has_high = me_slab < n_slab - 1
    first = me_seg == 0
    last = me_seg == n_seg - 1

    def span(c):
        return pl.ds(pl.multiple_of(c * size, size), size)

    def padded(c):
        return pl.ds(pl.multiple_of(c * size + PAD, 8), size)

    odd = lax.rem(me_slab, 2)

    def layer(j):
        return (1 - odd) * (layers - 1 - j) + odd * j

    close = layer(0)
    mids = [layer(j) for j in range(1, layers - 2)]
    next_far = layer(layers - 2)
    far = layer(layers - 1)
    mid_at = pl.ds(2 - odd, layers - 3)
    next_at = pl.ds(next_far, 1)
    close_at = pl.ds(close, 1)
    far_at = pl.ds(odd * (layers - 2), 2)

    near_at = pl.ds(2 * (1 - odd), layers - 2)

    begin = size + PAD
    later = min(begin + 2 * size, rows)
    pieces = ((0, begin), (begin, later - begin), (later, rows - later))

    def loads(j):
        at, count = pieces[j]
        here = pl.ds(at, count)
        return (
            pltpu.make_async_copy(
                cp.at[0, :, here], u0.at[pl.ds(1, layers), pl.ds(at + PAD, count)], sem_u0.at[j % 2]),
            pltpu.make_async_copy(ctl_in.at[0, :, here], ctl.at[:, here], sem_ctl.at[j % 2]),
            pltpu.make_async_copy(rate_in.at[:, here], rat.at[:, here], sem_rat.at[j % 2]),
        )

    has_far = jnp.logical_or(
        jnp.logical_and(has_low, odd == 0), jnp.logical_and(has_high, odd == 1))
    partner = {"slab": me_slab + 1 - 2 * odd}
    beyond = {"slab": me_slab - 1 + 2 * odd}

    def first_halo(j):
        at, count = pieces[j]
        return pltpu.make_async_remote_copy(
            cp.at[0, close, pl.ds(at, count)], u0.at[odd * top, pl.ds(at + PAD, count)],
            hs.at[0], hr_first.at[j], device_id=partner, device_id_type=MESH)

    def close_halo(k, buf, c):
        return pltpu.make_async_remote_copy(
            buf.at[close + 1, padded(c)], buf.at[odd * top, padded(c)],
            hs.at[0], hr_close.at[c], device_id=partner, device_id_type=MESH)

    def defect_halo(h):
        here = pl.ds(pl.multiple_of(h * (rows // HALVES) + PAD, 8), rows // HALVES)
        return pltpu.make_async_remote_copy(
            l2.at[close + 1, here], l2.at[odd * top, here],
            hs.at[0], hr_first.at[h], device_id=partner, device_id_type=MESH)

    def far_halo(k, buf, c):
        src = cp.at[0, far, span(c)] if buf is u0 else buf.at[far + 1, padded(c)]
        return pltpu.make_async_remote_copy(
            src, buf.at[(1 - odd) * top, padded(c)],
            hs.at[1], hr_far.at[k % 2, c], device_id=beyond, device_id_type=MESH)

    def send_first(j):
        first_halo(j).start()

    def wait_first(j):
        first_halo(j).wait_recv()

    def send_close(k, buf, c):
        close_halo(k, buf, c).start()

    def wait_close(k, buf, c):
        close_halo(k, buf, c).wait_recv()

    def send_far(k, buf, c):
        @pl.when(has_far)
        def _():
            far_halo(k, buf, c).start()

    def wait_far(k, buf, c):
        @pl.when(has_far)
        def _():
            far_halo(k, buf, c).wait_recv()

    def alt_c():
        return pltpu.make_async_copy(target, cpn, sem_alt)

    def alt_p():
        return pltpu.make_async_copy(cp.at[0], prior, sem_alt)

    def sent_halos():
        def taken(sem):
            four = u1.at[pl.ds(0, 4), pl.ds(0, rows)]
            pltpu.make_async_remote_copy(
                four, four, sem, hr_first.at[0],
                device_id=partner, device_id_type=MESH).wait_send()

        taken(hs.at[0])

        @pl.when(has_far)
        def _():
            taken(hs.at[1])

    rims = (0, layers - 1)

    def back(src, dst, sem):
        return pltpu.make_async_remote_copy(
            src, dst, zs.at[0], sem, device_id={"seg": me_seg - 1}, device_id_type=MESH)

    def onward(at, here, sem):
        return pltpu.make_async_remote_copy(
            end.at[at, here], prior.at[at, here], zs.at[1], sem,
            device_id={"seg": me_seg + 1}, device_id_type=MESH)

    def send_mid(c):
        return back(cp.at[0, mid_at, span(c)], cpn.at[mid_at, span(c)], zr_mid.at[c])

    def half(h):
        return pl.ds(pl.multiple_of(h * (rows // HALVES), 8), rows // HALVES)

    def send_rim(h, j):
        return back(cp.at[0, rims[j], half(h)], cpn.at[rims[j], half(h)], zr_rim.at[h])

    def both_rims(h):
        two = pl.ds(0, 2)
        return back(cp.at[0, two, half(h)], cpn.at[two, half(h)], zr_rim.at[h])

    def send_next(q):
        here = pl.ds(pl.multiple_of(q * (rows // QUARTERS), 8), rows // QUARTERS)
        return back(cp.at[0, next_at, here], cpn.at[next_at, here], zr_next.at[q])

    def send_far_end(c):
        return onward(far_at, span(c), zr_end.at[c])

    def send_near_end(at, r, count):
        return onward(at, pl.ds(pl.multiple_of(r, 8), count), zr_near)

    def all_near_ends():
        return onward(near_at, pl.ds(0, rows), zr_near)

    barrier = pltpu.get_barrier_semaphore()
    slab_peers = [{"slab": lax.rem(me_slab + d, n_slab)} for d in range(1, n_slab)]
    seg_peers = [{"seg": lax.rem(me_seg + d, n_seg)} for d in range(1, n_seg)]
    both = [
        {"seg": lax.rem(me_seg + e, n_seg), "slab": lax.rem(me_slab + d, n_slab)}
        for e in range(1, n_seg) for d in range(1, n_slab)
    ]
    direct = n_seg * n_slab <= 32
    near = slab_peers + seg_peers
    peers = near + both
    for peer in near:
        pl.semaphore_signal(barrier, inc=1, device_id=peer, device_id_type=MESH)

    for copy in loads(0):
        copy.start()

    pl.semaphore_wait(barrier, len(near))

    send_first(0)

    @pl.when(jnp.logical_not(first))
    def _():
        for j in range(2):
            send_rim(0, j).start()

    send_far(0, u0, 0)
    for copy in loads(1):
        copy.start()
    send_first(1)

    edge = jnp.zeros((PAD, cols), jnp.float32)
    for buf in (u0, u1, l2, l1):
        for z in range(1, top):
            buf[z, pl.ds(0, PAD), :] = edge
            buf[z, pl.ds(rows + PAD, PAD), :] = edge

    def clear(z):
        @pl.loop(0, rows // PAD)
        def _(i):
            for buf in (u0, u1, l2, l1):
                buf[z, pl.ds(pl.multiple_of(i * PAD + PAD, 8), PAD), :] = edge

    @pl.when(jnp.logical_not(has_low))
    def _():
        clear(0)

    @pl.when(jnp.logical_not(has_high))
    def _():
        clear(top)

    acc[...] = jnp.zeros_like(acc)

    lane = lax.broadcasted_iota(jnp.int32, (TILE, cols), 1)
    at_left = lane == 0
    at_right = lane == cols - 1

    def laplace(buf, z, r):
        tall = buf[z, pl.ds(pl.multiple_of(r - PAD, 8), TILE + 2 * PAD), :]
        mid = tall[PAD:PAD + TILE]
        beside = buf[z + 1, pl.ds(r, TILE), :] + buf[z - 1, pl.ds(r, TILE), :]
        beside = beside + (tall[PAD + 1:PAD + 1 + TILE] + tall[PAD - 1:PAD - 1 + TILE])
        right = jnp.where(at_right, 0.0, pltpu.roll(mid, cols - 1, 1))
        left = jnp.where(at_left, 0.0, pltpu.roll(mid, 1, 1))
        return mid, beside + (right + left) - 6.0 * mid

    def each_tile(c, body, zs, shift=0, count=tiles):
        def at_tile(i):
            r = pl.multiple_of(c * size + shift + i * TILE, 8)
            for z in zs:
                body(z, r, pl.ds(r, TILE), pl.multiple_of(r + PAD, 8))

        if len(zs) > 2:
            pl.loop(0, count)(at_tile)
        else:
            for i in range(count):
                at_tile(i)

    def add_square(v):
        sq = v * v
        part = sq[:PAD]
        for i in range(1, TILE // PAD):
            part = part + sq[i * PAD:(i + 1) * PAD]
        acc[...] = acc[...] + part

    def forward(src, c, dst, zs, shift=0, count=tiles):
        def body(z, r, at, p):
            u, lap = laplace(src, z + 1, p)
            new = u + 0.1 * (lap + rat[z, at, :] * u * (1.0 - u) + ctl[z, at, :])
            if dst is u1:
                u1[z + 1, pl.ds(p, TILE), :] = new
            else:
                end[z, at, :] = new
        each_tile(c, body, zs, shift, count)

    def between(i, low, high):
        return pl.when(jnp.logical_and(i >= low, i < high))

    @pl.loop(0, CHUNKS + LAG_U)
    def _(i):
        for j, step in enumerate((0, 1, 3)):
            @pl.when(i == step)
            def _():
                for copy in loads(j):
                    copy.wait()
                wait_first(j)

        @pl.when(i < CHUNKS)
        def _():
            forward(u0, i, u1, [close, *mids, next_far])
            send_close(1, u1, i)

        def do_mids(shift, count):
            forward(u1, i, end, mids, shift, count)

            @pl.when(jnp.logical_not(last))
            def _():
                send_near_end(mid_at, i * size + shift, count * TILE).start()

        @pl.when(i == 0)
        def _():
            do_mids(0, 1)
            for copy in loads(2):
                copy.start()
            send_first(2)

            @pl.loop(1, CHUNKS)
            def _(c):
                send_far(0, u0, c)

        @between(i, 1, CHUNKS)
        def _():
            do_mids(TILE - size, tiles)

        @pl.when(i == CHUNKS)
        def _():
            do_mids(TILE - size, tiles - 1)

        @pl.when(i == 1)
        def _():
            if direct:
                for peer in slab_peers:
                    pl.semaphore_signal(ready, inc=1, device_id=peer, device_id_type=MESH)

            @pl.when(last)
            def _():
                alt_c().start()

            @pl.when(first)
            def _():
                alt_p().start()

        @between(i, 2, CHUNKS + 2)
        def _():
            c = i - 2
            wait_close(1, u1, c)
            forward(u1, c, end, [close])

            @pl.when(jnp.logical_not(last))
            def _():
                send_near_end(close_at, c * size, size).start()

        @pl.when(jnp.logical_not(first))
        def _():
            for h in range(1, HALVES):
                @pl.when(i == h)
                def _():
                    for j in range(2):
                        send_rim(h, j).start()

            @between(i, HALVES, HALVES + QUARTERS)
            def _():
                send_next(i - HALVES).start()

            @pl.when(i >= LAG_U)
            def _():
                send_mid(i - LAG_U).start()

        @between(i, LAG_B, CHUNKS + LAG_B)
        def _():
            c = i - LAG_B
            wait_far(0, u0, c)
            forward(u0, c, u1, [far])
            send_far(1, u1, c)

        @pl.when(i >= LAG_U)
        def _():
            c = i - LAG_U
            wait_far(1, u1, c)
            forward(u1, c, end, [next_far, far])

            @pl.when(jnp.logical_not(last))
            def _():
                send_far_end(c).start()

    def defect(c, zs):
        def body(z, r, at, p):
            l2[z + 1, pl.ds(p, TILE), :] = end[z, at, :] - cpn[z, at, :]
        each_tile(c, body, zs)

    @pl.when(last)
    def _():
        alt_c().wait()

    @pl.when(first)
    def _():
        alt_p().wait()

    @pl.loop(0, CHUNKS)
    def _(c):
        @pl.when(jnp.logical_and(jnp.logical_not(last), lax.rem(c, CHUNKS // HALVES) == 0))
        def _():
            both_rims(c // (CHUNKS // HALVES)).wait_recv()
        defect(c, rims)
        send_far(2, l2, c)

        @pl.when(lax.rem(c, CHUNKS // HALVES) == CHUNKS // HALVES - 1)
        def _():
            defect_halo(c // (CHUNKS // HALVES)).start()

    def do_l1(c, zs):
        def body(z, r, at, p):
            lam, lap = laplace(l2, z + 1, p)
            new = lam + 0.1 * (lap + rat[z, at, :] * (1.0 - 2.0 * u1[z + 1, pl.ds(p, TILE), :]) * lam)
            l1[z + 1, pl.ds(p, TILE), :] = new
            g = 0.1 * (lam + new)
            gc[z, at, :] = g
            add_square(g)
        each_tile(c, body, zs)

    def do_l0(c, zs, whole=False):
        def body(z, r, at, p):
            lam, lap = laplace(l1, z + 1, p)
            start = u0[z + 1, pl.ds(p, TILE), :]
            g = lam + 0.1 * (lap + rat[z, at, :] * (1.0 - 2.0 * start) * lam)
            if whole:
                g = g - (prior[z, at, :] - start)
                add_square(g)
            gs[z, at, :] = g
        each_tile(c, body, zs)

    def do_start(c):
        @pl.when(jnp.logical_not(first))
        def _():
            send_far_end(c).wait_recv()

        def body(z, r, at, p):
            g = gs[z, at, :] - (prior[z, at, :] - u0[z + 1, pl.ds(p, TILE), :])
            gs[z, at, :] = g
            add_square(g)
        each_tile(c, body, [next_far, far])

    @pl.loop(0, CHUNKS)
    def _(c):
        @pl.when(jnp.logical_and(jnp.logical_not(last), lax.rem(c, CHUNKS // QUARTERS) == 0))
        def _():
            send_next(c // (CHUNKS // QUARTERS)).wait_recv()
        defect(c, [next_far])

        wait_far(2, l2, c)
        do_l1(c, [far])
        send_far(3, l1, c)

    @pl.when(jnp.logical_not(first))
    def _():
        all_near_ends().wait_recv()

    @pl.loop(0, CHUNKS + LAG_0)
    def _(i):
        @pl.when(i < CHUNKS)
        def _():
            @pl.when(jnp.logical_not(last))
            def _():
                send_mid(i).wait_recv()
            defect(i, mids)

            @pl.when(lax.rem(i, CHUNKS // HALVES) == 0)
            def _():
                defect_halo(i // (CHUNKS // HALVES)).wait_recv()
            do_l1(i, [close, next_far])
            send_close(3, l1, i)

        @between(i, 1, CHUNKS + 1)
        def _():
            do_l1(i - 1, mids)

        @pl.when(i < CHUNKS)
        def _():
            wait_far(3, l1, i)
            do_l0(i, [far])

        @between(i, 1, CHUNKS + 1)
        def _():
            do_l0(i - 1, [next_far])

        @pl.when(i >= LAG_0)
        def _():
            c = i - LAG_0
            wait_close(3, l1, c)
            do_l0(c, [close, *mids], True)
            do_start(c)

    def sent_all():
        sent_halos()

        @pl.when(jnp.logical_not(first))
        def _():
            back(cp.at[0], cpn, zr_mid.at[0]).wait_send()

        @pl.when(jnp.logical_not(last))
        def _():
            onward(pl.ds(0, layers), pl.ds(0, rows), zr_end.at[0]).wait_send()

    tile = acc[:, :128]
    for j in range(1, cols // 128):
        tile = tile + acc[:, j * 128:(j + 1) * 128]
    tile = jnp.sum(tile, axis=0, keepdims=True)

    def total(value, slots, owner, peers, ss, sr):
        count = len(peers)

        def copy(at, peer):
            return pltpu.make_async_remote_copy(
                slots.at[at], slots.at[at], ss, sr, device_id=peer, device_id_type=MESH)

        slots[owner] = value
        for peer in peers:
            copy(owner, peer).start()
        if slots is slot_a:
            sent_all()
        everything = copy(pl.ds(0, count), peers[0])
        everything.wait_recv()
        result = slots[0]
        for j in range(1, count + 1):
            result = result + slots[j]
        return result, everything

    if direct:
        pl.semaphore_wait(ready, len(slab_peers))
        tile, sent_a = total(tile, slot_a, me_seg * n_slab + me_slab, peers, as_, ar)
        sent = [sent_a]
    else:
        tile, sent_a = total(tile, slot_a, me_slab, slab_peers, as_, ar)
        tile, sent_b = total(tile, slot_b, me_seg, seg_peers, bs, br)
        sent = [sent_a, sent_b]
    tot_out[...] = tile
    for copies in sent:
        copies.wait_send()


def update_kernel(
    count, u0, ctl, gs, gc, tot, new_cp, new_ctl, out_a, out_b, sem_a, sem_b
):
    layers, rows, cols = ctl.shape
    size = rows // PARTS
    sum_of = jnp.sum(tot[...], axis=1, keepdims=True)
    scale = jnp.broadcast_to(0.5 / jnp.sqrt(sum_of / count + 1e-06), (PAD, cols))

    def save(c):
        at = pl.ds(pl.multiple_of(c * size, size), size)
        return (
            pltpu.make_async_copy(out_a.at[:, at], new_cp.at[0, :, at], sem_a),
            pltpu.make_async_copy(out_b.at[:, at], new_ctl.at[0, :, at], sem_b),
        )

    @pl.loop(0, PARTS)
    def _(c):
        @pl.loop(0, size // PAD)
        def _(i):
            r = pl.multiple_of(c * size + i * PAD, 8)
            at = pl.ds(r, PAD)
            for z in range(layers):
                start = u0[z + 1, pl.ds(pl.multiple_of(r + PAD, 8), PAD), :]
                out_a[z, at, :] = start - scale * gs[z, at, :]
                out_b[z, at, :] = ctl[z, at, :] - scale * gc[z, at, :]
        for copy in save(c):
            copy.start()

    pltpu.make_async_copy(out_a, new_cp.at[0], sem_a).wait()
    pltpu.make_async_copy(out_b, new_ctl.at[0], sem_b).wait()


def per_device(checkpoints, control, rate, target):
    n_seg = lax.axis_size("seg")
    n_slab = lax.axis_size("slab")
    layers, rows, cols = rate.shape
    f32 = jnp.float32
    block = pltpu.VMEM((layers, rows, cols), f32)
    wide = pltpu.VMEM((layers + 2, rows + 2 * PAD, cols), f32)
    dma = pltpu.SemaphoreType.DMA
    hbm = pl.BlockSpec(memory_space=pltpu.HBM)
    vmem = pl.BlockSpec(memory_space=pltpu.VMEM)
    kept = pl.pallas_call(
        functools.partial(kernel, n_seg, n_slab),
        out_shape=(wide, block, block, block, pltpu.VMEM((1, 128), f32)),
        in_specs=[hbm] * 4,
        out_specs=(vmem,) * 5,
        scratch_shapes=[
            wide, wide, wide,
            block, block, block, block,
            pltpu.VMEM((PAD, cols), f32),
            pltpu.VMEM((n_slab * n_seg, 1, 128), f32),
            pltpu.VMEM((n_seg, 1, 128), f32),
            dma((2,)), dma((2,)), dma((2,)),
            dma(()),
            dma((2,)), dma((3,)), dma((CHUNKS,)), dma((2, CHUNKS)),
            dma((2,)), dma((CHUNKS,)), dma(()), dma((CHUNKS,)), dma((HALVES,)), dma((QUARTERS,)),
            dma(()), dma(()), dma(()), dma(()),
            pltpu.SemaphoreType.REGULAR,
        ],
        compiler_params=pltpu.CompilerParams(
            collective_id=0, has_side_effects=True, vmem_limit_bytes=50 << 20
        ),
        name="shooting",
    )(checkpoints, control, rate, target)
    count = 2.0 * n_seg * n_slab * rate.size
    return pl.pallas_call(
        functools.partial(update_kernel, count),
        out_shape=(
            jax.ShapeDtypeStruct(checkpoints.shape, f32),
            jax.ShapeDtypeStruct(control.shape, f32),
        ),
        in_specs=[vmem] * 5,
        out_specs=(hbm, hbm),
        scratch_shapes=[block, block, dma(()), dma(())],
        compiler_params=pltpu.CompilerParams(vmem_limit_bytes=8 << 20),
        name="update",
    )(*kept)


def solution(mesh):
    return jax.shard_map(
        per_device,
        mesh=mesh,
        in_specs=(
            P("seg", "slab", None, None),
            P("seg", "slab", None, None),
            P("slab", None, None),
            P("slab", None, None),
        ),
        out_specs=(P("seg", "slab", None, None), P("seg", "slab", None, None)),
        check_vma=False,
    )
```

```python
import functools

import jax
import jax.numpy as jnp
from jax import lax
from jax.experimental import pallas as pl
from jax.experimental.pallas import tpu as pltpu
from jax.sharding import PartitionSpec as P

CHUNKS = 8
PARTS = 8
TILE = 16
PAD = 8
LAG_B = 2
LAG_U = 6
HALVES = 2
QUARTERS = 4
LAG_0 = 2
MESH = pl.DeviceIdType.MESH


def kernel(
    n_seg, n_slab,
    cp, ctl_in, rate_in, target,
    u0, ctl, gs, gc, tot_out,
    u1, l2, l1, rat, end, cpn, prior, acc, slot_a, slot_b,
    sem_u0, sem_ctl, sem_rat, sem_alt,
    hs, hr_first, hr_close, hr_far, zs, zr_end, zr_near, zr_mid, zr_rim, zr_next, as_, ar, bs, br,
    ready,
):
    me_seg = lax.axis_index("seg")
    me_slab = lax.axis_index("slab")
    layers, rows, cols = cp.shape[1:]
    size = rows // CHUNKS
    tiles = size // TILE
    top = layers + 1
    has_low = me_slab > 0
    has_high = me_slab < n_slab - 1
    first = me_seg == 0
    last = me_seg == n_seg - 1

    def span(c):
        return pl.ds(pl.multiple_of(c * size, size), size)

    def padded(c):
        return pl.ds(pl.multiple_of(c * size + PAD, 8), size)

    odd = lax.rem(me_slab, 2)

    def layer(j):
        return (1 - odd) * (layers - 1 - j) + odd * j

    close = layer(0)
    mids = [layer(j) for j in range(1, layers - 2)]
    next_far = layer(layers - 2)
    far = layer(layers - 1)
    mid_at = pl.ds(2 - odd, layers - 3)
    next_at = pl.ds(next_far, 1)
    close_at = pl.ds(close, 1)
    far_at = pl.ds(odd * (layers - 2), 2)

    near_at = pl.ds(2 * (1 - odd), layers - 2)

    begin = size + PAD
    later = min(begin + 2 * size, rows)
    pieces = ((0, begin), (begin, later - begin), (later, rows - later))

    def loads(j):
        at, count = pieces[j]
        here = pl.ds(at, count)
        return (
            pltpu.make_async_copy(
                cp.at[0, :, here], u0.at[pl.ds(1, layers), pl.ds(at + PAD, count)], sem_u0.at[j % 2]),
            pltpu.make_async_copy(ctl_in.at[0, :, here], ctl.at[:, here], sem_ctl.at[j % 2]),
            pltpu.make_async_copy(rate_in.at[:, here], rat.at[:, here], sem_rat.at[j % 2]),
        )

    has_far = jnp.logical_or(
        jnp.logical_and(has_low, odd == 0), jnp.logical_and(has_high, odd == 1))
    partner = {"slab": me_slab + 1 - 2 * odd}
    beyond = {"slab": me_slab - 1 + 2 * odd}

    def first_halo(j):
        at, count = pieces[j]
        return pltpu.make_async_remote_copy(
            cp.at[0, close, pl.ds(at, count)], u0.at[odd * top, pl.ds(at + PAD, count)],
            hs.at[0], hr_first.at[j], device_id=partner, device_id_type=MESH)

    def close_halo(k, buf, c):
        return pltpu.make_async_remote_copy(
            buf.at[close + 1, padded(c)], buf.at[odd * top, padded(c)],
            hs.at[0], hr_close.at[c], device_id=partner, device_id_type=MESH)

    def defect_halo(h):
        here = pl.ds(pl.multiple_of(h * (rows // HALVES) + PAD, 8), rows // HALVES)
        return pltpu.make_async_remote_copy(
            l2.at[close + 1, here], l2.at[odd * top, here],
            hs.at[0], hr_first.at[h], device_id=partner, device_id_type=MESH)

    def far_halo(k, buf, c):
        src = cp.at[0, far, span(c)] if buf is u0 else buf.at[far + 1, padded(c)]
        return pltpu.make_async_remote_copy(
            src, buf.at[(1 - odd) * top, padded(c)],
            hs.at[1], hr_far.at[k % 2, c], device_id=beyond, device_id_type=MESH)

    def send_first(j):
        first_halo(j).start()

    def wait_first(j):
        first_halo(j).wait_recv()

    def send_close(k, buf, c):
        close_halo(k, buf, c).start()

    def wait_close(k, buf, c):
        close_halo(k, buf, c).wait_recv()

    def send_far(k, buf, c):
        @pl.when(has_far)
        def _():
            far_halo(k, buf, c).start()

    def wait_far(k, buf, c):
        @pl.when(has_far)
        def _():
            far_halo(k, buf, c).wait_recv()

    def alt_c():
        return pltpu.make_async_copy(target, cpn, sem_alt)

    def alt_p():
        return pltpu.make_async_copy(cp.at[0], prior, sem_alt)

    def sent_halos():
        def taken(sem):
            four = u1.at[pl.ds(0, 4), pl.ds(0, rows)]
            pltpu.make_async_remote_copy(
                four, four, sem, hr_first.at[0],
                device_id=partner, device_id_type=MESH).wait_send()

        taken(hs.at[0])

        @pl.when(has_far)
        def _():
            taken(hs.at[1])

    rims = (0, layers - 1)

    def back(src, dst, sem):
        return pltpu.make_async_remote_copy(
            src, dst, zs.at[0], sem, device_id={"seg": me_seg - 1}, device_id_type=MESH)

    def onward(at, here, sem):
        return pltpu.make_async_remote_copy(
            end.at[at, here], prior.at[at, here], zs.at[1], sem,
            device_id={"seg": me_seg + 1}, device_id_type=MESH)

    def send_mid(c):
        return back(cp.at[0, mid_at, span(c)], cpn.at[mid_at, span(c)], zr_mid.at[c])

    def half(h):
        return pl.ds(pl.multiple_of(h * (rows // HALVES), 8), rows // HALVES)

    def send_rim(h, j):
        return back(cp.at[0, rims[j], half(h)], cpn.at[rims[j], half(h)], zr_rim.at[h])

    def both_rims(h):
        two = pl.ds(0, 2)
        return back(cp.at[0, two, half(h)], cpn.at[two, half(h)], zr_rim.at[h])

    def send_next(q):
        here = pl.ds(pl.multiple_of(q * (rows // QUARTERS), 8), rows // QUARTERS)
        return back(cp.at[0, next_at, here], cpn.at[next_at, here], zr_next.at[q])

    def send_far_end(c):
        return onward(far_at, span(c), zr_end.at[c])

    def send_near_end(at, r, count):
        return onward(at, pl.ds(pl.multiple_of(r, 8), count), zr_near)

    def all_near_ends():
        return onward(near_at, pl.ds(0, rows), zr_near)

    barrier = pltpu.get_barrier_semaphore()
    slab_peers = [{"slab": lax.rem(me_slab + d, n_slab)} for d in range(1, n_slab)]
    seg_peers = [{"seg": lax.rem(me_seg + d, n_seg)} for d in range(1, n_seg)]
    both = [
        {"seg": lax.rem(me_seg + e, n_seg), "slab": lax.rem(me_slab + d, n_slab)}
        for e in range(1, n_seg) for d in range(1, n_slab)
    ]
    direct = n_seg * n_slab <= 32
    near = slab_peers + seg_peers
    peers = near + both
    for peer in near:
        pl.semaphore_signal(barrier, inc=1, device_id=peer, device_id_type=MESH)

    for copy in loads(0):
        copy.start()

    pl.semaphore_wait(barrier, len(near))

    send_first(0)

    @pl.when(jnp.logical_not(first))
    def _():
        for j in range(2):
            send_rim(0, j).start()

    send_far(0, u0, 0)
    for copy in loads(1):
        copy.start()
    send_first(1)

    edge = jnp.zeros((PAD, cols), jnp.float32)
    for buf in (u0, u1, l2, l1):
        for z in range(1, top):
            buf[z, pl.ds(0, PAD), :] = edge
            buf[z, pl.ds(rows + PAD, PAD), :] = edge

    def clear(z):
        @pl.loop(0, rows // PAD)
        def _(i):
            for buf in (u0, u1, l2, l1):
                buf[z, pl.ds(pl.multiple_of(i * PAD + PAD, 8), PAD), :] = edge

    @pl.when(jnp.logical_not(has_low))
    def _():
        clear(0)

    @pl.when(jnp.logical_not(has_high))
    def _():
        clear(top)

    acc[...] = jnp.zeros_like(acc)

    lane = lax.broadcasted_iota(jnp.int32, (TILE, cols), 1)
    at_left = lane == 0
    at_right = lane == cols - 1

    def laplace(buf, z, r):
        tall = buf[z, pl.ds(pl.multiple_of(r - PAD, 8), TILE + 2 * PAD), :]
        mid = tall[PAD:PAD + TILE]
        beside = buf[z + 1, pl.ds(r, TILE), :] + buf[z - 1, pl.ds(r, TILE), :]
        beside = beside + (tall[PAD + 1:PAD + 1 + TILE] + tall[PAD - 1:PAD - 1 + TILE])
        right = jnp.where(at_right, 0.0, pltpu.roll(mid, cols - 1, 1))
        left = jnp.where(at_left, 0.0, pltpu.roll(mid, 1, 1))
        return mid, beside + (right + left) - 6.0 * mid

    def each_tile(c, body, zs, shift=0, count=tiles):
        def at_tile(i):
            r = pl.multiple_of(c * size + shift + i * TILE, 8)
            for z in zs:
                body(z, r, pl.ds(r, TILE), pl.multiple_of(r + PAD, 8))

        if len(zs) > 3:
            pl.loop(0, count)(at_tile)
        else:
            for i in range(count):
                at_tile(i)

    def add_square(v):
        sq = v * v
        part = sq[:PAD]
        for i in range(1, TILE // PAD):
            part = part + sq[i * PAD:(i + 1) * PAD]
        acc[...] = acc[...] + part

    def forward(src, c, dst, zs, shift=0, count=tiles):
        def body(z, r, at, p):
            u, lap = laplace(src, z + 1, p)
            new = u + 0.1 * (lap + rat[z, at, :] * u * (1.0 - u) + ctl[z, at, :])
            if dst is u1:
                u1[z + 1, pl.ds(p, TILE), :] = new
            else:
                end[z, at, :] = new
        each_tile(c, body, zs, shift, count)

    def between(i, low, high):
        return pl.when(jnp.logical_and(i >= low, i < high))

    @pl.loop(0, CHUNKS + LAG_U)
    def _(i):
        for j, step in enumerate((0, 1, 3)):
            @pl.when(i == step)
            def _():
                for copy in loads(j):
                    copy.wait()
                wait_first(j)

        @pl.when(i < CHUNKS)
        def _():
            forward(u0, i, u1, [close, *mids, next_far])
            send_close(1, u1, i)

        def do_mids(shift, count):
            forward(u1, i, end, mids, shift, count)

            @pl.when(jnp.logical_not(last))
            def _():
                send_near_end(mid_at, i * size + shift, count * TILE).start()

        @pl.when(i == 0)
        def _():
            do_mids(0, 1)
            for copy in loads(2):
                copy.start()
            send_first(2)

            @pl.loop(1, CHUNKS)
            def _(c):
                send_far(0, u0, c)

        @between(i, 1, CHUNKS)
        def _():
            do_mids(TILE - size, tiles)

        @pl.when(i == CHUNKS)
        def _():
            do_mids(TILE - size, tiles - 1)

        @pl.when(i == 1)
        def _():
            if direct:
                for peer in slab_peers:
                    pl.semaphore_signal(ready, inc=1, device_id=peer, device_id_type=MESH)

            @pl.when(last)
            def _():
                alt_c().start()

            @pl.when(first)
            def _():
                alt_p().start()

        @between(i, 2, CHUNKS + 2)
        def _():
            c = i - 2
            wait_close(1, u1, c)
            forward(u1, c, end, [close])

            @pl.when(jnp.logical_not(last))
            def _():
                send_near_end(close_at, c * size, size).start()

        @pl.when(jnp.logical_not(first))
        def _():
            for h in range(1, HALVES):
                @pl.when(i == h)
                def _():
                    for j in range(2):
                        send_rim(h, j).start()

            @between(i, HALVES, HALVES + QUARTERS)
            def _():
                send_next(i - HALVES).start()

            @pl.when(i >= LAG_U)
            def _():
                send_mid(i - LAG_U).start()

        @between(i, LAG_B, CHUNKS + LAG_B)
        def _():
            c = i - LAG_B
            wait_far(0, u0, c)
            forward(u0, c, u1, [far])
            send_far(1, u1, c)

        @pl.when(i >= LAG_U)
        def _():
            c = i - LAG_U
            wait_far(1, u1, c)
            forward(u1, c, end, [next_far, far])

            @pl.when(jnp.logical_not(last))
            def _():
                send_far_end(c).start()

    def defect(c, zs):
        def body(z, r, at, p):
            l2[z + 1, pl.ds(p, TILE), :] = end[z, at, :] - cpn[z, at, :]
        each_tile(c, body, zs)

    @pl.when(last)
    def _():
        alt_c().wait()

    @pl.when(first)
    def _():
        alt_p().wait()

    @pl.loop(0, CHUNKS)
    def _(c):
        @pl.when(jnp.logical_and(jnp.logical_not(last), lax.rem(c, CHUNKS // HALVES) == 0))
        def _():
            both_rims(c // (CHUNKS // HALVES)).wait_recv()
        defect(c, rims)
        send_far(2, l2, c)

        @pl.when(lax.rem(c, CHUNKS // HALVES) == CHUNKS // HALVES - 1)
        def _():
            defect_halo(c // (CHUNKS // HALVES)).start()

    def do_l1(c, zs):
        def body(z, r, at, p):
            lam, lap = laplace(l2, z + 1, p)
            new = lam + 0.1 * (lap + rat[z, at, :] * (1.0 - 2.0 * u1[z + 1, pl.ds(p, TILE), :]) * lam)
            l1[z + 1, pl.ds(p, TILE), :] = new
            g = 0.1 * (lam + new)
            gc[z, at, :] = g
            add_square(g)
        each_tile(c, body, zs)

    def do_l0(c, zs, whole=False):
        def body(z, r, at, p):
            lam, lap = laplace(l1, z + 1, p)
            start = u0[z + 1, pl.ds(p, TILE), :]
            g = lam + 0.1 * (lap + rat[z, at, :] * (1.0 - 2.0 * start) * lam)
            if whole:
                g = g - (prior[z, at, :] - start)
                add_square(g)
            gs[z, at, :] = g
        each_tile(c, body, zs)

    def do_start(c):
        @pl.when(jnp.logical_not(first))
        def _():
            send_far_end(c).wait_recv()

        def body(z, r, at, p):
            g = gs[z, at, :] - (prior[z, at, :] - u0[z + 1, pl.ds(p, TILE), :])
            gs[z, at, :] = g
            add_square(g)
        each_tile(c, body, [next_far, far])

    @pl.loop(0, CHUNKS)
    def _(c):
        @pl.when(jnp.logical_and(jnp.logical_not(last), lax.rem(c, CHUNKS // QUARTERS) == 0))
        def _():
            send_next(c // (CHUNKS // QUARTERS)).wait_recv()
        defect(c, [next_far])

        wait_far(2, l2, c)
        do_l1(c, [far])
        send_far(3, l1, c)

    @pl.when(jnp.logical_not(first))
    def _():
        all_near_ends().wait_recv()

    @pl.loop(0, CHUNKS + LAG_0)
    def _(i):
        @pl.when(i < CHUNKS)
        def _():
            @pl.when(jnp.logical_not(last))
            def _():
                send_mid(i).wait_recv()
            defect(i, mids)

            @pl.when(lax.rem(i, CHUNKS // HALVES) == 0)
            def _():
                defect_halo(i // (CHUNKS // HALVES)).wait_recv()
            do_l1(i, [close, next_far])
            send_close(3, l1, i)

        @between(i, 1, CHUNKS + 1)
        def _():
            do_l1(i - 1, mids)

        @pl.when(i < CHUNKS)
        def _():
            wait_far(3, l1, i)
            do_l0(i, [far])

        @between(i, 1, CHUNKS + 1)
        def _():
            do_l0(i - 1, [next_far])

        @pl.when(i >= LAG_0)
        def _():
            c = i - LAG_0
            wait_close(3, l1, c)
            do_l0(c, [close, *mids], True)
            do_start(c)

    def sent_all():
        sent_halos()

        @pl.when(jnp.logical_not(first))
        def _():
            back(cp.at[0], cpn, zr_mid.at[0]).wait_send()

        @pl.when(jnp.logical_not(last))
        def _():
            onward(pl.ds(0, layers), pl.ds(0, rows), zr_end.at[0]).wait_send()

    tile = acc[:, :128]
    for j in range(1, cols // 128):
        tile = tile + acc[:, j * 128:(j + 1) * 128]
    tile = jnp.sum(tile, axis=0, keepdims=True)

    def total(value, slots, owner, peers, ss, sr):
        count = len(peers)

        def copy(at, peer):
            return pltpu.make_async_remote_copy(
                slots.at[at], slots.at[at], ss, sr, device_id=peer, device_id_type=MESH)

        slots[owner] = value
        for peer in peers:
            copy(owner, peer).start()
        if slots is slot_a:
            sent_all()
        everything = copy(pl.ds(0, count), peers[0])
        everything.wait_recv()
        result = slots[0]
        for j in range(1, count + 1):
            result = result + slots[j]
        return result, everything

    if direct:
        pl.semaphore_wait(ready, len(slab_peers))
        tile, sent_a = total(tile, slot_a, me_seg * n_slab + me_slab, peers, as_, ar)
        sent = [sent_a]
    else:
        tile, sent_a = total(tile, slot_a, me_slab, slab_peers, as_, ar)
        tile, sent_b = total(tile, slot_b, me_seg, seg_peers, bs, br)
        sent = [sent_a, sent_b]
    tot_out[...] = tile
    for copies in sent:
        copies.wait_send()


def update_kernel(
    count, u0, ctl, gs, gc, tot, new_cp, new_ctl, out_a, out_b, sem_a, sem_b
):
    layers, rows, cols = ctl.shape
    size = rows // PARTS
    sum_of = jnp.sum(tot[...], axis=1, keepdims=True)
    scale = jnp.broadcast_to(0.5 / jnp.sqrt(sum_of / count + 1e-06), (PAD, cols))

    def save(c):
        at = pl.ds(pl.multiple_of(c * size, size), size)
        return (
            pltpu.make_async_copy(out_a.at[:, at], new_cp.at[0, :, at], sem_a),
            pltpu.make_async_copy(out_b.at[:, at], new_ctl.at[0, :, at], sem_b),
        )

    @pl.loop(0, PARTS)
    def _(c):
        @pl.loop(0, size // PAD)
        def _(i):
            r = pl.multiple_of(c * size + i * PAD, 8)
            at = pl.ds(r, PAD)
            for z in range(layers):
                start = u0[z + 1, pl.ds(pl.multiple_of(r + PAD, 8), PAD), :]
                out_a[z, at, :] = start - scale * gs[z, at, :]
                out_b[z, at, :] = ctl[z, at, :] - scale * gc[z, at, :]
        for copy in save(c):
            copy.start()

    pltpu.make_async_copy(out_a, new_cp.at[0], sem_a).wait()
    pltpu.make_async_copy(out_b, new_ctl.at[0], sem_b).wait()


def per_device(checkpoints, control, rate, target):
    n_seg = lax.axis_size("seg")
    n_slab = lax.axis_size("slab")
    layers, rows, cols = rate.shape
    f32 = jnp.float32
    block = pltpu.VMEM((layers, rows, cols), f32)
    wide = pltpu.VMEM((layers + 2, rows + 2 * PAD, cols), f32)
    dma = pltpu.SemaphoreType.DMA
    hbm = pl.BlockSpec(memory_space=pltpu.HBM)
    vmem = pl.BlockSpec(memory_space=pltpu.VMEM)
    kept = pl.pallas_call(
        functools.partial(kernel, n_seg, n_slab),
        out_shape=(wide, block, block, block, pltpu.VMEM((1, 128), f32)),
        in_specs=[hbm] * 4,
        out_specs=(vmem,) * 5,
        scratch_shapes=[
            wide, wide, wide,
            block, block, block, block,
            pltpu.VMEM((PAD, cols), f32),
            pltpu.VMEM((n_slab * n_seg, 1, 128), f32),
            pltpu.VMEM((n_seg, 1, 128), f32),
            dma((2,)), dma((2,)), dma((2,)),
            dma(()),
            dma((2,)), dma((3,)), dma((CHUNKS,)), dma((2, CHUNKS)),
            dma((2,)), dma((CHUNKS,)), dma(()), dma((CHUNKS,)), dma((HALVES,)), dma((QUARTERS,)),
            dma(()), dma(()), dma(()), dma(()),
            pltpu.SemaphoreType.REGULAR,
        ],
        compiler_params=pltpu.CompilerParams(
            collective_id=0, has_side_effects=True, vmem_limit_bytes=50 << 20
        ),
        name="shooting",
    )(checkpoints, control, rate, target)
    count = 2.0 * n_seg * n_slab * rate.size
    return pl.pallas_call(
        functools.partial(update_kernel, count),
        out_shape=(
            jax.ShapeDtypeStruct(checkpoints.shape, f32),
            jax.ShapeDtypeStruct(control.shape, f32),
        ),
        in_specs=[vmem] * 5,
        out_specs=(hbm, hbm),
        scratch_shapes=[block, block, dma(()), dma(())],
        compiler_params=pltpu.CompilerParams(vmem_limit_bytes=8 << 20),
        name="update",
    )(*kept)


def solution(mesh):
    return jax.shard_map(
        per_device,
        mesh=mesh,
        in_specs=(
            P("seg", "slab", None, None),
            P("seg", "slab", None, None),
            P("slab", None, None),
            P("slab", None, None),
        ),
        out_specs=(P("seg", "slab", None, None), P("seg", "slab", None, None)),
        check_vma=False,
    )
```

```python
import functools

import jax
import jax.numpy as jnp
from jax import lax
from jax.experimental import pallas as pl
from jax.experimental.pallas import tpu as pltpu
from jax.sharding import PartitionSpec as P

CHUNKS = 8
PARTS = 8
TILE = 16
PAD = 8
LAG_B = 2
LAG_U = 6
HALVES = 2
QUARTERS = 4
LAG_0 = 2
MESH = pl.DeviceIdType.MESH


def kernel(
    n_seg, n_slab,
    cp, ctl_in, rate_in, target,
    u0, ctl, gs, gc, tot_out,
    u1, l2, l1, rat, end, cpn, prior, acc, slot_a, slot_b,
    sem_u0, sem_ctl, sem_rat, sem_alt_c, sem_alt_p,
    hs, hr_first, hr_close, hr_far, zs, zr_end, zr_near, zr_mid, zr_rim, zr_next, as_, ar, bs, br,
    ready,
):
    me_seg = lax.axis_index("seg")
    me_slab = lax.axis_index("slab")
    layers, rows, cols = cp.shape[1:]
    size = rows // CHUNKS
    tiles = size // TILE
    top = layers + 1
    has_low = me_slab > 0
    has_high = me_slab < n_slab - 1
    first = me_seg == 0
    last = me_seg == n_seg - 1

    def span(c):
        return pl.ds(pl.multiple_of(c * size, size), size)

    def padded(c):
        return pl.ds(pl.multiple_of(c * size + PAD, 8), size)

    odd = lax.rem(me_slab, 2)

    def layer(j):
        return (1 - odd) * (layers - 1 - j) + odd * j

    close = layer(0)
    mids = [layer(j) for j in range(1, layers - 2)]
    next_far = layer(layers - 2)
    far = layer(layers - 1)
    mid_at = pl.ds(2 - odd, layers - 3)
    next_at = pl.ds(next_far, 1)
    close_at = pl.ds(close, 1)
    far_at = pl.ds(odd * (layers - 2), 2)

    near_at = pl.ds(2 * (1 - odd), layers - 2)

    begin = size + PAD
    later = min(begin + 2 * size, rows)
    pieces = ((0, begin), (begin, later - begin), (later, rows - later))

    def loads(j):
        at, count = pieces[j]
        here = pl.ds(at, count)
        return (
            pltpu.make_async_copy(
                cp.at[0, :, here], u0.at[pl.ds(1, layers), pl.ds(at + PAD, count)], sem_u0.at[j % 2]),
            pltpu.make_async_copy(ctl_in.at[0, :, here], ctl.at[:, here], sem_ctl.at[j % 2]),
            pltpu.make_async_copy(rate_in.at[:, here], rat.at[:, here], sem_rat.at[j % 2]),
        )

    has_far = jnp.logical_or(
        jnp.logical_and(has_low, odd == 0), jnp.logical_and(has_high, odd == 1))
    partner = {"slab": me_slab + 1 - 2 * odd}
    beyond = {"slab": me_slab - 1 + 2 * odd}

    def first_halo(j):
        at, count = pieces[j]
        return pltpu.make_async_remote_copy(
            cp.at[0, close, pl.ds(at, count)], u0.at[odd * top, pl.ds(at + PAD, count)],
            hs.at[0], hr_first.at[j], device_id=partner, device_id_type=MESH)

    def close_halo(k, buf, c):
        return pltpu.make_async_remote_copy(
            buf.at[close + 1, padded(c)], buf.at[odd * top, padded(c)],
            hs.at[0], hr_close.at[k % 2, c], device_id=partner, device_id_type=MESH)

    def far_halo(k, buf, c):
        src = cp.at[0, far, span(c)] if buf is u0 else buf.at[far + 1, padded(c)]
        return pltpu.make_async_remote_copy(
            src, buf.at[(1 - odd) * top, padded(c)],
            hs.at[1], hr_far.at[k % 2, c], device_id=beyond, device_id_type=MESH)

    def send_first(j):
        first_halo(j).start()

    def wait_first(j):
        first_halo(j).wait_recv()

    def send_close(k, buf, c):
        close_halo(k, buf, c).start()

    def wait_close(k, buf, c):
        close_halo(k, buf, c).wait_recv()

    def send_far(k, buf, c):
        @pl.when(has_far)
        def _():
            far_halo(k, buf, c).start()

    def wait_far(k, buf, c):
        @pl.when(has_far)
        def _():
            far_halo(k, buf, c).wait_recv()

    def alt_c():
        return pltpu.make_async_copy(target, cpn, sem_alt_c)

    def alt_p():
        return pltpu.make_async_copy(cp.at[0], prior, sem_alt_p)

    def sent_halos():
        def taken(sem):
            four = u1.at[pl.ds(0, 4), pl.ds(0, rows)]
            pltpu.make_async_remote_copy(
                four, four, sem, hr_first.at[0],
                device_id=partner, device_id_type=MESH).wait_send()

        taken(hs.at[0])

        @pl.when(has_far)
        def _():
            taken(hs.at[1])

    rims = (0, layers - 1)

    def back(src, dst, sem):
        return pltpu.make_async_remote_copy(
            src, dst, zs.at[0], sem, device_id={"seg": me_seg - 1}, device_id_type=MESH)

    def onward(at, here, sem):
        return pltpu.make_async_remote_copy(
            end.at[at, here], prior.at[at, here], zs.at[1], sem,
            device_id={"seg": me_seg + 1}, device_id_type=MESH)

    def send_mid(c):
        return back(cp.at[0, mid_at, span(c)], cpn.at[mid_at, span(c)], zr_mid.at[c])

    def half(h):
        return pl.ds(pl.multiple_of(h * (rows // HALVES), 8), rows // HALVES)

    def send_rim(h, j):
        return back(cp.at[0, rims[j], half(h)], cpn.at[rims[j], half(h)], zr_rim.at[h])

    def both_rims(h):
        two = pl.ds(0, 2)
        return back(cp.at[0, two, half(h)], cpn.at[two, half(h)], zr_rim.at[h])

    def send_next(q):
        here = pl.ds(pl.multiple_of(q * (rows // QUARTERS), 8), rows // QUARTERS)
        return back(cp.at[0, next_at, here], cpn.at[next_at, here], zr_next.at[q])

    def send_far_end(c):
        return onward(far_at, span(c), zr_end.at[c])

    def send_near_end(at, r, count):
        return onward(at, pl.ds(pl.multiple_of(r, 8), count), zr_near)

    def all_near_ends():
        return onward(near_at, pl.ds(0, rows), zr_near)

    barrier = pltpu.get_barrier_semaphore()
    slab_peers = [{"slab": lax.rem(me_slab + d, n_slab)} for d in range(1, n_slab)]
    seg_peers = [{"seg": lax.rem(me_seg + d, n_seg)} for d in range(1, n_seg)]
    both = [
        {"seg": lax.rem(me_seg + e, n_seg), "slab": lax.rem(me_slab + d, n_slab)}
        for e in range(1, n_seg) for d in range(1, n_slab)
    ]
    direct = n_seg * n_slab <= 32
    near = slab_peers + seg_peers
    peers = near + both
    for peer in near:
        pl.semaphore_signal(barrier, inc=1, device_id=peer, device_id_type=MESH)

    for copy in loads(0):
        copy.start()

    pl.semaphore_wait(barrier, len(near))

    send_first(0)

    @pl.when(jnp.logical_not(first))
    def _():
        for j in range(2):
            send_rim(0, j).start()

    send_far(0, u0, 0)
    for copy in loads(1):
        copy.start()
    send_first(1)

    edge = jnp.zeros((PAD, cols), jnp.float32)
    for buf in (u0, u1, l2, l1):
        for z in range(1, top):
            buf[z, pl.ds(0, PAD), :] = edge
            buf[z, pl.ds(rows + PAD, PAD), :] = edge

    def clear(z):
        @pl.loop(0, rows // PAD)
        def _(i):
            for buf in (u0, u1, l2, l1):
                buf[z, pl.ds(pl.multiple_of(i * PAD + PAD, 8), PAD), :] = edge

    @pl.when(jnp.logical_not(has_low))
    def _():
        clear(0)

    @pl.when(jnp.logical_not(has_high))
    def _():
        clear(top)

    acc[...] = jnp.zeros_like(acc)

    lane = lax.broadcasted_iota(jnp.int32, (TILE, cols), 1)
    at_left = lane == 0
    at_right = lane == cols - 1

    def laplace(buf, z, r):
        tall = buf[z, pl.ds(pl.multiple_of(r - PAD, 8), TILE + 2 * PAD), :]
        mid = tall[PAD:PAD + TILE]
        beside = buf[z + 1, pl.ds(r, TILE), :] + buf[z - 1, pl.ds(r, TILE), :]
        beside = beside + (tall[PAD + 1:PAD + 1 + TILE] + tall[PAD - 1:PAD - 1 + TILE])
        right = jnp.where(at_right, 0.0, pltpu.roll(mid, cols - 1, 1))
        left = jnp.where(at_left, 0.0, pltpu.roll(mid, 1, 1))
        return mid, beside + (right + left) - 6.0 * mid

    def each_tile(c, body, zs, shift=0, count=tiles):
        def at_tile(i):
            r = pl.multiple_of(c * size + shift + i * TILE, 8)
            for z in zs:
                body(z, r, pl.ds(r, TILE), pl.multiple_of(r + PAD, 8))

        if len(zs) > 2:
            pl.loop(0, count)(at_tile)
        else:
            for i in range(count):
                at_tile(i)

    def add_square(v):
        sq = v * v
        part = sq[:PAD]
        for i in range(1, TILE // PAD):
            part = part + sq[i * PAD:(i + 1) * PAD]
        acc[...] = acc[...] + part

    def forward(src, c, dst, zs, shift=0, count=tiles):
        def body(z, r, at, p):
            u, lap = laplace(src, z + 1, p)
            new = u + 0.1 * (lap + rat[z, at, :] * u * (1.0 - u) + ctl[z, at, :])
            if dst is u1:
                u1[z + 1, pl.ds(p, TILE), :] = new
            else:
                end[z, at, :] = new
        each_tile(c, body, zs, shift, count)

    def between(i, low, high):
        return pl.when(jnp.logical_and(i >= low, i < high))

    @pl.loop(0, CHUNKS + LAG_U)
    def _(i):
        for j, step in enumerate((0, 1, 3)):
            @pl.when(i == step)
            def _():
                for copy in loads(j):
                    copy.wait()
                wait_first(j)

        @pl.when(i < CHUNKS)
        def _():
            forward(u0, i, u1, [close, *mids, next_far])
            send_close(1, u1, i)

        def do_mids(shift, count):
            forward(u1, i, end, mids, shift, count)

            @pl.when(jnp.logical_not(last))
            def _():
                send_near_end(mid_at, i * size + shift, count * TILE).start()

        @pl.when(i == 0)
        def _():
            do_mids(0, 1)
            for copy in loads(2):
                copy.start()
            send_first(2)

            @pl.loop(1, CHUNKS)
            def _(c):
                send_far(0, u0, c)

        @between(i, 1, CHUNKS)
        def _():
            do_mids(TILE - size, tiles)

        @pl.when(i == CHUNKS)
        def _():
            do_mids(TILE - size, tiles - 1)

        @pl.when(i == 1)
        def _():
            if direct:
                for peer in slab_peers:
                    pl.semaphore_signal(ready, inc=1, device_id=peer, device_id_type=MESH)

            @pl.when(last)
            def _():
                alt_c().start()

            @pl.when(first)
            def _():
                alt_p().start()

        @between(i, 2, CHUNKS + 2)
        def _():
            c = i - 2
            wait_close(1, u1, c)
            forward(u1, c, end, [close])

            @pl.when(jnp.logical_not(last))
            def _():
                send_near_end(close_at, c * size, size).start()

        @pl.when(jnp.logical_not(first))
        def _():
            for h in range(1, HALVES):
                @pl.when(i == h)
                def _():
                    for j in range(2):
                        send_rim(h, j).start()

            @between(i, HALVES, HALVES + QUARTERS)
            def _():
                send_next(i - HALVES).start()

            @pl.when(i >= LAG_U)
            def _():
                send_mid(i - LAG_U).start()

        @between(i, LAG_B, CHUNKS + LAG_B)
        def _():
            c = i - LAG_B
            wait_far(0, u0, c)
            forward(u0, c, u1, [far])
            send_far(1, u1, c)

        @pl.when(i >= LAG_U)
        def _():
            c = i - LAG_U
            wait_far(1, u1, c)
            forward(u1, c, end, [next_far, far])

            @pl.when(jnp.logical_not(last))
            def _():
                send_far_end(c).start()

    def defect(c, zs):
        def body(z, r, at, p):
            l2[z + 1, pl.ds(p, TILE), :] = end[z, at, :] - cpn[z, at, :]
        each_tile(c, body, zs)

    @pl.when(last)
    def _():
        alt_c().wait()

    @pl.when(first)
    def _():
        alt_p().wait()

    @pl.loop(0, CHUNKS)
    def _(c):
        @pl.when(jnp.logical_and(jnp.logical_not(last), lax.rem(c, CHUNKS // HALVES) == 0))
        def _():
            both_rims(c // (CHUNKS // HALVES)).wait_recv()
        defect(c, rims)
        send_far(2, l2, c)
        send_close(2, l2, c)

    def do_l1(c, zs):
        def body(z, r, at, p):
            lam, lap = laplace(l2, z + 1, p)
            new = lam + 0.1 * (lap + rat[z, at, :] * (1.0 - 2.0 * u1[z + 1, pl.ds(p, TILE), :]) * lam)
            l1[z + 1, pl.ds(p, TILE), :] = new
            g = 0.1 * (lam + new)
            gc[z, at, :] = g
            add_square(g)
        each_tile(c, body, zs)

    def do_l0(c, zs, whole=False):
        def body(z, r, at, p):
            lam, lap = laplace(l1, z + 1, p)
            start = u0[z + 1, pl.ds(p, TILE), :]
            g = lam + 0.1 * (lap + rat[z, at, :] * (1.0 - 2.0 * start) * lam)
            if whole:
                g = g - (prior[z, at, :] - start)
                add_square(g)
            gs[z, at, :] = g
        each_tile(c, body, zs)

    def do_start(c):
        @pl.when(jnp.logical_not(first))
        def _():
            send_far_end(c).wait_recv()

        def body(z, r, at, p):
            g = gs[z, at, :] - (prior[z, at, :] - u0[z + 1, pl.ds(p, TILE), :])
            gs[z, at, :] = g
            add_square(g)
        each_tile(c, body, [next_far, far])

    @pl.loop(0, CHUNKS)
    def _(c):
        @pl.when(jnp.logical_and(jnp.logical_not(last), lax.rem(c, CHUNKS // QUARTERS) == 0))
        def _():
            send_next(c // (CHUNKS // QUARTERS)).wait_recv()
        defect(c, [next_far])

        wait_far(2, l2, c)
        do_l1(c, [far])
        send_far(3, l1, c)

    @pl.when(jnp.logical_not(first))
    def _():
        all_near_ends().wait_recv()

    @pl.loop(0, CHUNKS + LAG_0)
    def _(i):
        @pl.when(i < CHUNKS)
        def _():
            @pl.when(jnp.logical_not(last))
            def _():
                send_mid(i).wait_recv()
            defect(i, mids)
            wait_close(2, l2, i)
            do_l1(i, [close, next_far])
            send_close(3, l1, i)

        @between(i, 1, CHUNKS + 1)
        def _():
            do_l1(i - 1, mids)

        @pl.when(i < CHUNKS)
        def _():
            wait_far(3, l1, i)
            do_l0(i, [far])

        @between(i, 1, CHUNKS + 1)
        def _():
            do_l0(i - 1, [next_far])

        @pl.when(i >= LAG_0)
        def _():
            c = i - LAG_0
            wait_close(3, l1, c)
            do_l0(c, [close, *mids], True)
            do_start(c)

    def sent_all():
        sent_halos()

        @pl.when(jnp.logical_not(first))
        def _():
            back(cp.at[0], cpn, zr_mid.at[0]).wait_send()

        @pl.when(jnp.logical_not(last))
        def _():
            onward(pl.ds(0, layers), pl.ds(0, rows), zr_end.at[0]).wait_send()

    tile = acc[:, :128]
    for j in range(1, cols // 128):
        tile = tile + acc[:, j * 128:(j + 1) * 128]
    tile = jnp.sum(tile, axis=0, keepdims=True)

    def total(value, slots, owner, peers, ss, sr, order=None):
        count = len(peers)

        def copy(at, peer):
            return pltpu.make_async_remote_copy(
                slots.at[at], slots.at[at], ss, sr, device_id=peer, device_id_type=MESH)

        slots[owner] = value
        if order is None:
            for peer in peers:
                copy(owner, peer).start()
        else:
            for j, peer in enumerate(order):
                @pl.when(owner != j)
                def _():
                    copy(owner, peer).start()
        if slots is slot_a:
            sent_all()
        everything = copy(pl.ds(0, count), peers[0])
        everything.wait_recv()
        result = slots[0]
        for j in range(1, count + 1):
            result = result + slots[j]
        return result, everything

    if direct:
        pl.semaphore_wait(ready, len(slab_peers))
        everyone = [{"seg": e, "slab": d} for e in range(n_seg) for d in range(n_slab)]
        tile, sent_a = total(
            tile, slot_a, me_seg * n_slab + me_slab, peers, as_, ar, everyone)
        sent = [sent_a]
    else:
        tile, sent_a = total(tile, slot_a, me_slab, slab_peers, as_, ar)
        tile, sent_b = total(tile, slot_b, me_seg, seg_peers, bs, br)
        sent = [sent_a, sent_b]
    tot_out[...] = tile
    for copies in sent:
        copies.wait_send()


def update_kernel(
    count, u0, ctl, gs, gc, tot, new_cp, new_ctl, out_a, out_b, sem_a, sem_b
):
    layers, rows, cols = ctl.shape
    size = rows // PARTS
    sum_of = jnp.sum(tot[...], axis=1, keepdims=True)
    scale = jnp.broadcast_to(0.5 / jnp.sqrt(sum_of / count + 1e-06), (PAD, cols))

    def save(c):
        at = pl.ds(pl.multiple_of(c * size, size), size)
        return (
            pltpu.make_async_copy(out_a.at[:, at], new_cp.at[0, :, at], sem_a),
            pltpu.make_async_copy(out_b.at[:, at], new_ctl.at[0, :, at], sem_b),
        )

    @pl.loop(0, PARTS)
    def _(c):
        @pl.loop(0, size // PAD)
        def _(i):
            r = pl.multiple_of(c * size + i * PAD, 8)
            at = pl.ds(r, PAD)
            for z in range(layers):
                start = u0[z + 1, pl.ds(pl.multiple_of(r + PAD, 8), PAD), :]
                out_a[z, at, :] = start - scale * gs[z, at, :]
                out_b[z, at, :] = ctl[z, at, :] - scale * gc[z, at, :]
        for copy in save(c):
            copy.start()

    pltpu.make_async_copy(out_a, new_cp.at[0], sem_a).wait()
    pltpu.make_async_copy(out_b, new_ctl.at[0], sem_b).wait()


def per_device(checkpoints, control, rate, target):
    n_seg = lax.axis_size("seg")
    n_slab = lax.axis_size("slab")
    layers, rows, cols = rate.shape
    f32 = jnp.float32
    block = pltpu.VMEM((layers, rows, cols), f32)
    wide = pltpu.VMEM((layers + 2, rows + 2 * PAD, cols), f32)
    dma = pltpu.SemaphoreType.DMA
    hbm = pl.BlockSpec(memory_space=pltpu.HBM)
    vmem = pl.BlockSpec(memory_space=pltpu.VMEM)
    kept = pl.pallas_call(
        functools.partial(kernel, n_seg, n_slab),
        out_shape=(wide, block, block, block, pltpu.VMEM((1, 128), f32)),
        in_specs=[hbm] * 4,
        out_specs=(vmem,) * 5,
        scratch_shapes=[
            wide, wide, wide,
            block, block, block, block,
            pltpu.VMEM((PAD, cols), f32),
            pltpu.VMEM((n_slab * n_seg, 1, 128), f32),
            pltpu.VMEM((n_seg, 1, 128), f32),
            dma((2,)), dma((2,)), dma((2,)),
            dma(()), dma(()),
            dma((2,)), dma((3,)), dma((2, CHUNKS)), dma((2, CHUNKS)),
            dma((2,)), dma((CHUNKS,)), dma(()), dma((CHUNKS,)), dma((HALVES,)), dma((QUARTERS,)),
            dma(()), dma(()), dma(()), dma(()),
            pltpu.SemaphoreType.REGULAR,
        ],
        compiler_params=pltpu.CompilerParams(
            collective_id=0, has_side_effects=True, vmem_limit_bytes=50 << 20
        ),
        name="shooting",
    )(checkpoints, control, rate, target)
    count = 2.0 * n_seg * n_slab * rate.size
    return pl.pallas_call(
        functools.partial(update_kernel, count),
        out_shape=(
            jax.ShapeDtypeStruct(checkpoints.shape, f32),
            jax.ShapeDtypeStruct(control.shape, f32),
        ),
        in_specs=[vmem] * 5,
        out_specs=(hbm, hbm),
        scratch_shapes=[block, block, dma(()), dma(())],
        compiler_params=pltpu.CompilerParams(vmem_limit_bytes=8 << 20),
        name="update",
    )(*kept)


def solution(mesh):
    return jax.shard_map(
        per_device,
        mesh=mesh,
        in_specs=(
            P("seg", "slab", None, None),
            P("seg", "slab", None, None),
            P("slab", None, None),
            P("slab", None, None),
        ),
        out_specs=(P("seg", "slab", None, None), P("seg", "slab", None, None)),
        check_vma=False,
    )
```

```python
import functools

import jax
import jax.numpy as jnp
from jax import lax
from jax.experimental import pallas as pl
from jax.experimental.pallas import tpu as pltpu
from jax.sharding import PartitionSpec as P

CHUNKS = 8
PARTS = 8
TILE = 16
PAD = 8
LAG_B = 2
LAG_U = 6
HALVES = 2
QUARTERS = 4
LAG_0 = 2
MESH = pl.DeviceIdType.MESH


def kernel(
    n_seg, n_slab,
    cp, ctl_in, rate_in, target,
    u0, ctl, gs, gc, tot_out,
    u1, l2, l1, rat, end, cpn, prior, acc, slot_a, slot_b,
    sem_u0, sem_ctl, sem_rat, sem_alt,
    hs, hr_first, hr_close, hr_far, zs, zr_end, zr_near, zr_mid, zr_rim, zr_next, as_, ar, bs, br,
    ready,
):
    me_seg = lax.axis_index("seg")
    me_slab = lax.axis_index("slab")
    layers, rows, cols = cp.shape[1:]
    size = rows // CHUNKS
    tiles = size // TILE
    top = layers + 1
    has_low = me_slab > 0
    has_high = me_slab < n_slab - 1
    first = me_seg == 0
    last = me_seg == n_seg - 1

    def span(c):
        return pl.ds(pl.multiple_of(c * size, size), size)

    def padded(c):
        return pl.ds(pl.multiple_of(c * size + PAD, 8), size)

    odd = lax.rem(me_slab, 2)

    def layer(j):
        return (1 - odd) * (layers - 1 - j) + odd * j

    close = layer(0)
    mids = [layer(j) for j in range(1, layers - 2)]
    next_far = layer(layers - 2)
    far = layer(layers - 1)
    mid_at = pl.ds(2 - odd, layers - 3)
    next_at = pl.ds(next_far, 1)
    close_at = pl.ds(close, 1)
    far_at = pl.ds(odd * (layers - 2), 2)

    near_at = pl.ds(2 * (1 - odd), layers - 2)

    begin = size + PAD
    later = min(begin + 2 * size, rows)
    pieces = ((0, begin), (begin, later - begin), (later, rows - later))

    def loads(j):
        at, count = pieces[j]
        here = pl.ds(at, count)
        return (
            pltpu.make_async_copy(
                cp.at[0, :, here], u0.at[pl.ds(1, layers), pl.ds(at + PAD, count)], sem_u0.at[j % 2]),
            pltpu.make_async_copy(ctl_in.at[0, :, here], ctl.at[:, here], sem_ctl.at[j % 2]),
            pltpu.make_async_copy(rate_in.at[:, here], rat.at[:, here], sem_rat.at[j % 2]),
        )

    has_far = jnp.logical_or(
        jnp.logical_and(has_low, odd == 0), jnp.logical_and(has_high, odd == 1))
    partner = {"slab": me_slab + 1 - 2 * odd}
    beyond = {"slab": me_slab - 1 + 2 * odd}

    def first_halo(j):
        at, count = pieces[j]
        return pltpu.make_async_remote_copy(
            cp.at[0, close, pl.ds(at, count)], u0.at[odd * top, pl.ds(at + PAD, count)],
            hs.at[0], hr_first.at[j], device_id=partner, device_id_type=MESH)

    def close_halo(k, buf, c):
        return pltpu.make_async_remote_copy(
            buf.at[close + 1, padded(c)], buf.at[odd * top, padded(c)],
            hs.at[0], hr_close.at[c], device_id=partner, device_id_type=MESH)

    def defect_halo(h):
        here = pl.ds(pl.multiple_of(h * (rows // HALVES) + PAD, 8), rows // HALVES)
        return pltpu.make_async_remote_copy(
            l2.at[close + 1, here], l2.at[odd * top, here],
            hs.at[0], hr_first.at[h], device_id=partner, device_id_type=MESH)

    def far_halo(k, buf, c):
        return pltpu.make_async_remote_copy(
            buf.at[far + 1, padded(c)], buf.at[(1 - odd) * top, padded(c)],
            hs.at[1], hr_far.at[k % 2, c], device_id=beyond, device_id_type=MESH)

    def first_far(q):
        here = rows // QUARTERS
        return pltpu.make_async_remote_copy(
            cp.at[0, far, pl.ds(pl.multiple_of(q * here, 8), here)],
            u0.at[(1 - odd) * top, pl.ds(pl.multiple_of(q * here + PAD, 8), here)],
            hs.at[1], hr_far.at[0, q], device_id=beyond, device_id_type=MESH)

    def send_first(j):
        first_halo(j).start()

    def wait_first(j):
        first_halo(j).wait_recv()

    def send_close(k, buf, c):
        close_halo(k, buf, c).start()

    def wait_close(k, buf, c):
        close_halo(k, buf, c).wait_recv()

    def send_far(k, buf, c):
        @pl.when(has_far)
        def _():
            far_halo(k, buf, c).start()

    def wait_far(k, buf, c):
        @pl.when(has_far)
        def _():
            far_halo(k, buf, c).wait_recv()

    def alt_c():
        return pltpu.make_async_copy(target, cpn, sem_alt)

    def alt_p():
        return pltpu.make_async_copy(cp.at[0], prior, sem_alt)

    def sent_halos():
        def taken(sem):
            four = u1.at[pl.ds(0, 4), pl.ds(0, rows)]
            pltpu.make_async_remote_copy(
                four, four, sem, hr_first.at[0],
                device_id=partner, device_id_type=MESH).wait_send()

        taken(hs.at[0])

        @pl.when(has_far)
        def _():
            taken(hs.at[1])

    rims = (0, layers - 1)

    def back(src, dst, sem):
        return pltpu.make_async_remote_copy(
            src, dst, zs.at[0], sem, device_id={"seg": me_seg - 1}, device_id_type=MESH)

    def onward(at, here, sem):
        return pltpu.make_async_remote_copy(
            end.at[at, here], prior.at[at, here], zs.at[1], sem,
            device_id={"seg": me_seg + 1}, device_id_type=MESH)

    def send_mid(c):
        return back(cp.at[0, mid_at, span(c)], cpn.at[mid_at, span(c)], zr_mid.at[c])

    def half(h):
        return pl.ds(pl.multiple_of(h * (rows // HALVES), 8), rows // HALVES)

    def send_rim(h, j):
        return back(cp.at[0, rims[j], half(h)], cpn.at[rims[j], half(h)], zr_rim.at[h])

    def both_rims(h):
        two = pl.ds(0, 2)
        return back(cp.at[0, two, half(h)], cpn.at[two, half(h)], zr_rim.at[h])

    def send_next(q):
        here = pl.ds(pl.multiple_of(q * (rows // QUARTERS), 8), rows // QUARTERS)
        return back(cp.at[0, next_at, here], cpn.at[next_at, here], zr_next.at[q])

    def send_far_end(c):
        return onward(far_at, span(c), zr_end.at[c])

    def send_near_end(at, r, count):
        return onward(at, pl.ds(pl.multiple_of(r, 8), count), zr_near)

    def all_near_ends():
        return onward(near_at, pl.ds(0, rows), zr_near)

    barrier = pltpu.get_barrier_semaphore()
    slab_peers = [{"slab": lax.rem(me_slab + d, n_slab)} for d in range(1, n_slab)]
    seg_peers = [{"seg": lax.rem(me_seg + d, n_seg)} for d in range(1, n_seg)]
    both = [
        {"seg": lax.rem(me_seg + e, n_seg), "slab": lax.rem(me_slab + d, n_slab)}
        for e in range(1, n_seg) for d in range(1, n_slab)
    ]
    direct = n_seg * n_slab <= 32
    near = slab_peers + seg_peers
    peers = near + both
    for peer in near:
        pl.semaphore_signal(barrier, inc=1, device_id=peer, device_id_type=MESH)

    for copy in loads(0):
        copy.start()

    pl.semaphore_wait(barrier, len(near))

    send_first(0)

    @pl.when(jnp.logical_not(first))
    def _():
        for j in range(2):
            send_rim(0, j).start()

    @pl.when(has_far)
    def _():
        first_far(0).start()

    for copy in loads(1):
        copy.start()
    send_first(1)

    edge = jnp.zeros((PAD, cols), jnp.float32)
    for buf in (u0, u1, l2, l1):
        for z in range(1, top):
            buf[z, pl.ds(0, PAD), :] = edge
            buf[z, pl.ds(rows + PAD, PAD), :] = edge

    def clear(z):
        @pl.loop(0, rows // PAD)
        def _(i):
            for buf in (u0, u1, l2, l1):
                buf[z, pl.ds(pl.multiple_of(i * PAD + PAD, 8), PAD), :] = edge

    @pl.when(jnp.logical_not(has_low))
    def _():
        clear(0)

    @pl.when(jnp.logical_not(has_high))
    def _():
        clear(top)

    acc[...] = jnp.zeros_like(acc)

    lane = lax.broadcasted_iota(jnp.int32, (TILE, cols), 1)
    at_left = lane == 0
    at_right = lane == cols - 1

    def laplace(buf, z, r):
        tall = buf[z, pl.ds(pl.multiple_of(r - PAD, 8), TILE + 2 * PAD), :]
        mid = tall[PAD:PAD + TILE]
        beside = buf[z + 1, pl.ds(r, TILE), :] + buf[z - 1, pl.ds(r, TILE), :]
        beside = beside + (tall[PAD + 1:PAD + 1 + TILE] + tall[PAD - 1:PAD - 1 + TILE])
        right = jnp.where(at_right, 0.0, pltpu.roll(mid, cols - 1, 1))
        left = jnp.where(at_left, 0.0, pltpu.roll(mid, 1, 1))
        return mid, beside + (right + left) - 6.0 * mid

    def each_tile(c, body, zs, shift=0, count=tiles):
        def at_tile(i):
            r = pl.multiple_of(c * size + shift + i * TILE, 8)
            for z in zs:
                body(z, r, pl.ds(r, TILE), pl.multiple_of(r + PAD, 8))

        if len(zs) > 2:
            pl.loop(0, count)(at_tile)
        else:
            for i in range(count):
                at_tile(i)

    def add_square(v):
        sq = v * v
        part = sq[:PAD]
        for i in range(1, TILE // PAD):
            part = part + sq[i * PAD:(i + 1) * PAD]
        acc[...] = acc[...] + part

    def forward(src, c, dst, zs, shift=0, count=tiles):
        def body(z, r, at, p):
            u, lap = laplace(src, z + 1, p)
            new = u + 0.1 * (lap + rat[z, at, :] * u * (1.0 - u) + ctl[z, at, :])
            if dst is u1:
                u1[z + 1, pl.ds(p, TILE), :] = new
            else:
                end[z, at, :] = new
        each_tile(c, body, zs, shift, count)

    def between(i, low, high):
        return pl.when(jnp.logical_and(i >= low, i < high))

    @pl.loop(0, CHUNKS + LAG_U)
    def _(i):
        for j, step in enumerate((0, 1, 3)):
            @pl.when(i == step)
            def _():
                for copy in loads(j):
                    copy.wait()
                wait_first(j)

        @pl.when(i < CHUNKS)
        def _():
            forward(u0, i, u1, [close, *mids, next_far])
            send_close(1, u1, i)

        def do_mids(shift, count):
            forward(u1, i, end, mids, shift, count)

            @pl.when(jnp.logical_not(last))
            def _():
                send_near_end(mid_at, i * size + shift, count * TILE).start()

        @pl.when(i == 0)
        def _():
            do_mids(0, 1)
            for copy in loads(2):
                copy.start()
            send_first(2)

            @pl.when(has_far)
            def _():
                for q in range(1, QUARTERS):
                    first_far(q).start()

        @between(i, 1, CHUNKS)
        def _():
            do_mids(TILE - size, tiles)

        @pl.when(i == CHUNKS)
        def _():
            do_mids(TILE - size, tiles - 1)

        @pl.when(i == 1)
        def _():
            if direct:
                for peer in slab_peers:
                    pl.semaphore_signal(ready, inc=1, device_id=peer, device_id_type=MESH)

            @pl.when(last)
            def _():
                alt_c().start()

            @pl.when(first)
            def _():
                alt_p().start()

        @between(i, 2, CHUNKS + 2)
        def _():
            c = i - 2
            wait_close(1, u1, c)
            forward(u1, c, end, [close])

            @pl.when(jnp.logical_not(last))
            def _():
                send_near_end(close_at, c * size, size).start()

        @pl.when(jnp.logical_not(first))
        def _():
            for h in range(1, HALVES):
                @pl.when(i == h)
                def _():
                    for j in range(2):
                        send_rim(h, j).start()

            @between(i, HALVES, HALVES + QUARTERS)
            def _():
                send_next(i - HALVES).start()

            @pl.when(i >= LAG_U)
            def _():
                send_mid(i - LAG_U).start()

        @between(i, LAG_B, CHUNKS + LAG_B)
        def _():
            c = i - LAG_B

            @pl.when(jnp.logical_and(has_far, lax.rem(c, CHUNKS // QUARTERS) == 0))
            def _():
                first_far(c // (CHUNKS // QUARTERS)).wait_recv()
            forward(u0, c, u1, [far])
            send_far(1, u1, c)

        @pl.when(i >= LAG_U)
        def _():
            c = i - LAG_U
            wait_far(1, u1, c)
            forward(u1, c, end, [next_far, far])

            @pl.when(jnp.logical_not(last))
            def _():
                send_far_end(c).start()

    def defect(c, zs):
        def body(z, r, at, p):
            l2[z + 1, pl.ds(p, TILE), :] = end[z, at, :] - cpn[z, at, :]
        each_tile(c, body, zs)

    @pl.when(last)
    def _():
        alt_c().wait()

    @pl.when(first)
    def _():
        alt_p().wait()

    @pl.loop(0, CHUNKS)
    def _(c):
        @pl.when(jnp.logical_and(jnp.logical_not(last), lax.rem(c, CHUNKS // HALVES) == 0))
        def _():
            both_rims(c // (CHUNKS // HALVES)).wait_recv()
        defect(c, rims)
        send_far(2, l2, c)

        @pl.when(lax.rem(c, CHUNKS // HALVES) == CHUNKS // HALVES - 1)
        def _():
            defect_halo(c // (CHUNKS // HALVES)).start()

    def do_l1(c, zs):
        def body(z, r, at, p):
            lam, lap = laplace(l2, z + 1, p)
            new = lam + 0.1 * (lap + rat[z, at, :] * (1.0 - 2.0 * u1[z + 1, pl.ds(p, TILE), :]) * lam)
            l1[z + 1, pl.ds(p, TILE), :] = new
            g = 0.1 * (lam + new)
            gc[z, at, :] = g
            add_square(g)
        each_tile(c, body, zs)

    def do_l0(c, zs, whole=False):
        def body(z, r, at, p):
            lam, lap = laplace(l1, z + 1, p)
            start = u0[z + 1, pl.ds(p, TILE), :]
            g = lam + 0.1 * (lap + rat[z, at, :] * (1.0 - 2.0 * start) * lam)
            if whole:
                g = g - (prior[z, at, :] - start)
                add_square(g)
            gs[z, at, :] = g
        each_tile(c, body, zs)

    def do_start(c):
        @pl.when(jnp.logical_not(first))
        def _():
            send_far_end(c).wait_recv()

        def body(z, r, at, p):
            g = gs[z, at, :] - (prior[z, at, :] - u0[z + 1, pl.ds(p, TILE), :])
            gs[z, at, :] = g
            add_square(g)
        each_tile(c, body, [next_far, far])

    @pl.loop(0, CHUNKS)
    def _(c):
        @pl.when(jnp.logical_and(jnp.logical_not(last), lax.rem(c, CHUNKS // QUARTERS) == 0))
        def _():
            send_next(c // (CHUNKS // QUARTERS)).wait_recv()
        defect(c, [next_far])

        wait_far(2, l2, c)
        do_l1(c, [far])
        send_far(3, l1, c)

    @pl.when(jnp.logical_not(first))
    def _():
        all_near_ends().wait_recv()

    @pl.loop(0, CHUNKS + LAG_0)
    def _(i):
        @pl.when(i < CHUNKS)
        def _():
            @pl.when(jnp.logical_not(last))
            def _():
                send_mid(i).wait_recv()
            defect(i, mids)

            @pl.when(lax.rem(i, CHUNKS // HALVES) == 0)
            def _():
                defect_halo(i // (CHUNKS // HALVES)).wait_recv()
            do_l1(i, [close, next_far])
            send_close(3, l1, i)

        @between(i, 1, CHUNKS + 1)
        def _():
            do_l1(i - 1, mids)

        @pl.when(i < CHUNKS)
        def _():
            wait_far(3, l1, i)
            do_l0(i, [far])

        @between(i, 1, CHUNKS + 1)
        def _():
            do_l0(i - 1, [next_far])

        @pl.when(i >= LAG_0)
        def _():
            c = i - LAG_0
            wait_close(3, l1, c)
            do_l0(c, [close, *mids], True)
            do_start(c)

    def sent_all():
        sent_halos()

        @pl.when(jnp.logical_not(first))
        def _():
            back(cp.at[0], cpn, zr_mid.at[0]).wait_send()

        @pl.when(jnp.logical_not(last))
        def _():
            onward(pl.ds(0, layers), pl.ds(0, rows), zr_end.at[0]).wait_send()

    tile = acc[:, :128]
    for j in range(1, cols // 128):
        tile = tile + acc[:, j * 128:(j + 1) * 128]
    tile = jnp.sum(tile, axis=0, keepdims=True)

    def total(value, slots, owner, peers, ss, sr):
        count = len(peers)

        def copy(at, peer):
            return pltpu.make_async_remote_copy(
                slots.at[at], slots.at[at], ss, sr, device_id=peer, device_id_type=MESH)

        slots[owner] = value
        for peer in peers:
            copy(owner, peer).start()
        if slots is slot_a:
            sent_all()
        everything = copy(pl.ds(0, count), peers[0])
        everything.wait_recv()
        result = slots[0]
        for j in range(1, count + 1):
            result = result + slots[j]
        return result, everything

    if direct:
        pl.semaphore_wait(ready, len(slab_peers))
        tile, sent_a = total(tile, slot_a, me_seg * n_slab + me_slab, peers, as_, ar)
        sent = [sent_a]
    else:
        tile, sent_a = total(tile, slot_a, me_slab, slab_peers, as_, ar)
        tile, sent_b = total(tile, slot_b, me_seg, seg_peers, bs, br)
        sent = [sent_a, sent_b]
    tot_out[...] = tile
    for copies in sent:
        copies.wait_send()


def update_kernel(
    count, u0, ctl, gs, gc, tot, new_cp, new_ctl, out_a, out_b, sem_a, sem_b
):
    layers, rows, cols = ctl.shape
    size = rows // PARTS
    sum_of = jnp.sum(tot[...], axis=1, keepdims=True)
    scale = jnp.broadcast_to(0.5 / jnp.sqrt(sum_of / count + 1e-06), (PAD, cols))

    def save(c):
        at = pl.ds(pl.multiple_of(c * size, size), size)
        return (
            pltpu.make_async_copy(out_a.at[:, at], new_cp.at[0, :, at], sem_a),
            pltpu.make_async_copy(out_b.at[:, at], new_ctl.at[0, :, at], sem_b),
        )

    @pl.loop(0, PARTS)
    def _(c):
        @pl.loop(0, size // PAD)
        def _(i):
            r = pl.multiple_of(c * size + i * PAD, 8)
            at = pl.ds(r, PAD)
            for z in range(layers):
                start = u0[z + 1, pl.ds(pl.multiple_of(r + PAD, 8), PAD), :]
                out_a[z, at, :] = start - scale * gs[z, at, :]
                out_b[z, at, :] = ctl[z, at, :] - scale * gc[z, at, :]
        for copy in save(c):
            copy.start()

    pltpu.make_async_copy(out_a, new_cp.at[0], sem_a).wait()
    pltpu.make_async_copy(out_b, new_ctl.at[0], sem_b).wait()


def per_device(checkpoints, control, rate, target):
    n_seg = lax.axis_size("seg")
    n_slab = lax.axis_size("slab")
    layers, rows, cols = rate.shape
    f32 = jnp.float32
    block = pltpu.VMEM((layers, rows, cols), f32)
    wide = pltpu.VMEM((layers + 2, rows + 2 * PAD, cols), f32)
    dma = pltpu.SemaphoreType.DMA
    hbm = pl.BlockSpec(memory_space=pltpu.HBM)
    vmem = pl.BlockSpec(memory_space=pltpu.VMEM)
    kept = pl.pallas_call(
        functools.partial(kernel, n_seg, n_slab),
        out_shape=(wide, block, block, block, pltpu.VMEM((1, 128), f32)),
        in_specs=[hbm] * 4,
        out_specs=(vmem,) * 5,
        scratch_shapes=[
            wide, wide, wide,
            block, block, block, block,
            pltpu.VMEM((PAD, cols), f32),
            pltpu.VMEM((n_slab * n_seg, 1, 128), f32),
            pltpu.VMEM((n_seg, 1, 128), f32),
            dma((2,)), dma((2,)), dma((2,)),
            dma(()),
            dma((2,)), dma((3,)), dma((CHUNKS,)), dma((2, CHUNKS)),
            dma((2,)), dma((CHUNKS,)), dma(()), dma((CHUNKS,)), dma((HALVES,)), dma((QUARTERS,)),
            dma(()), dma(()), dma(()), dma(()),
            pltpu.SemaphoreType.REGULAR,
        ],
        compiler_params=pltpu.CompilerParams(
            collective_id=0, has_side_effects=True, vmem_limit_bytes=50 << 20
        ),
        name="shooting",
    )(checkpoints, control, rate, target)
    count = 2.0 * n_seg * n_slab * rate.size
    return pl.pallas_call(
        functools.partial(update_kernel, count),
        out_shape=(
            jax.ShapeDtypeStruct(checkpoints.shape, f32),
            jax.ShapeDtypeStruct(control.shape, f32),
        ),
        in_specs=[vmem] * 5,
        out_specs=(hbm, hbm),
        scratch_shapes=[block, block, dma(()), dma(())],
        compiler_params=pltpu.CompilerParams(vmem_limit_bytes=8 << 20),
        name="update",
    )(*kept)


def solution(mesh):
    return jax.shard_map(
        per_device,
        mesh=mesh,
        in_specs=(
            P("seg", "slab", None, None),
            P("seg", "slab", None, None),
            P("slab", None, None),
            P("slab", None, None),
        ),
        out_specs=(P("seg", "slab", None, None), P("seg", "slab", None, None)),
        check_vma=False,
    )
```
